32 devices in a mesh: replica: 8 (over y, x, core), tok: 4 (over z).
Axes of the slice: x: 2, y: 2, z: 4, core: 2. Of those that a mesh axis runs over, the one named last changes fastest.
Arguments:
- activations: bfloat16 [8192, 2880], P(('replica', 'tok')), may hold values from -6 to 6
- cotangent: bfloat16 [8192, 512], P(('replica', 'tok')), may hold values from -6 to 6
- next_inputs: bfloat16 [8192, 2880], P(('replica', 'tok')), may hold values from -6 to 6
- weight_tiles: bfloat16 [360, 4096], P('tok'), may hold values from -0.109375 to 0.109375
- momentum: float32 [8, 360, 4096], P('replica', 'tok'), may hold values from -6 to 6
- chosen: int32 [8, 4, 8], P('replica', 'tok'), may hold values from 0 to 89, as said below
- counts: int32 [8, 4], P('replica', 'tok'), may hold values from 1 to 8, as said below
Outputs:
- values: bfloat16 [8192, 512], P(('replica', 'tok'))
- new_momentum: float32 [8, 360, 4096], P('replica', 'tok')
The draws below stay inside these ranges and needn't reach their ends.
Inputs may be any that keep to these rules, and one draw needn't show every extreme that they name: Each list chosen[r, k] names 8 different tile numbers of the shard's 90 tiles; only the first counts[r, k] of them are selected. `counts`: in every draw some token shard has 8 selected tiles in every replica.
All inputs are finite; a program needn't handle non-finite values.
Results may differ from the reference program's by a relative error of at most 0.015.
Values may be sent and summed in bfloat16 or wider, within the bound.
No kernel may reach another device: no remote copies, remote signals or barrier semaphores. Data moves between devices by JAX's collectives and lax.ppermute only.
A program may use at most 64 MiB of HBM per device.

```python
import math
import jax
import jax.numpy as jnp
from jax import lax

D = 2880
KV = 512
TOK_DEV = 256
TILE = 64
KEEP = 32
SLOTS = 8
REPLICAS = 8
TOK_SHARDS = 4
ROWS_REP = 1024
ROWS_ALL = 8192
TILES = 360
TILES_DEV = 90


def draw_chosen(key, part):
    scores = jax.random.randint(jax.random.fold_in(key, 11), (REPLICAS, TOK_SHARDS, TILES_DEV), 0, 1 << 20)
    scores = scores * TILES_DEV + jnp.arange(TILES_DEV, dtype=jnp.int32)
    order = jnp.argsort(scores, axis=-1)
    return order[:, :, :SLOTS].astype(jnp.int32)


def draw_counts(key, part):
    spread = jax.random.randint(jax.random.fold_in(key, 23), (REPLICAS, TOK_SHARDS), 1, SLOTS + 1)
    busiest = jax.random.randint(jax.random.fold_in(key, 29), (), 0, TOK_SHARDS)
    filled = jnp.arange(TOK_SHARDS, dtype=jnp.int32)[None, :] == busiest
    return jnp.where(filled, SLOTS, spread).astype(jnp.int32)


def strengthened(values, rng, source, target, blocks, factor):
    def block_of(axis_at):
        return (jnp.arange(values.shape[axis_at]) // (values.shape[axis_at] // blocks)).reshape((-1,) + (1,) * (values.ndim - 1 - axis_at))

    near = jax.random.permutation(rng, blocks)[block_of(target)]
    far = (block_of(target) + blocks // 2) % blocks
    return jnp.where((block_of(source) == near) | (block_of(source) == far), factor * values, values)


def block_levels(own_key, shape, split, low, top_value):
    loudness = 1.0
    for dim, parts in split:
        heights = jax.random.uniform(jax.random.fold_in(jax.random.fold_in(own_key, 6), dim), (parts,), jnp.float32, low / len(split), top_value / len(split))
        loudness = loudness * jnp.repeat(jnp.exp(heights), shape[dim] // parts).reshape((-1,) + (1,) * (len(shape) - 1 - dim))
    return loudness


def scatter_about(own_key, dims, width, bound, split=(), held_as=jnp.bfloat16):
    factor_of = block_levels(own_key, dims, split, -0.22, 0.18) if split else 1.0
    array = jax.random.normal(own_key, dims, jnp.float32) * width * factor_of
    return jnp.minimum(jnp.maximum(array, -bound), bound).astype(held_as)


def heavy_noise(key, extent, scale, reach, shards, heavy, kind=jnp.bfloat16):
    result = scale * jax.random.normal(key, extent, jnp.float32)
    if shards:
        result = result * block_levels(key, extent, shards, -0.22, 0.18)
    return jnp.clip(strengthened(result, jax.random.fold_in(key, 3), *heavy), -reach, reach).astype(kind)


def setup_inputs(seed: int = 0) -> dict:
    seeds = jax.random.split(jax.random.key(seed), 8)
    activations = heavy_noise(seeds[0], (ROWS_ALL, D), 1.0, 6.0, ((0, 32),), (0, 1, 32, 2.75))
    cotangent = scatter_about(seeds[1], (ROWS_ALL, KV), 1.0, 6.0, ((0, 32),))
    next_inputs = scatter_about(seeds[2], (ROWS_ALL, D), 1.0, 6.0, ((0, 32),))
    weight_tiles = scatter_about(seeds[3], (TILES, TILE * TILE), D ** -0.5, 0.109375, ((0, 4),))
    momentum = scatter_about(seeds[4], (REPLICAS, TILES, TILE * TILE), 1.0, 6.0, ((0, 8), (1, 4)), jnp.float32)
    chosen = draw_chosen(jax.random.fold_in(seeds[7], 71), 0)
    counts = draw_counts(jax.random.fold_in(seeds[7], 71), 0)
    return dict(activations=activations, cotangent=cotangent, next_inputs=next_inputs, weight_tiles=weight_tiles, momentum=momentum, chosen=chosen, counts=counts)


momentum_decay = 0.9
step_size = 0.01

def cosine_rows(count):
    frequency = jnp.arange(count, dtype=jnp.float32)[:, None]
    position = jnp.arange(TILE, dtype=jnp.float32)[None, :]
    cosines = jnp.cos(math.pi * (2.0 * position + 1.0) * frequency / (2.0 * TILE))
    factor = jnp.where(frequency == 0, math.sqrt(1.0 / TILE), math.sqrt(2.0 / TILE))
    return (cosines * factor).astype(jnp.float32)

def to_tiles(matrix):
    row_tiles = matrix.shape[0] // TILE
    col_tiles = matrix.shape[1] // TILE
    shaped = matrix.reshape(row_tiles, TILE, col_tiles, TILE).transpose(0, 2, 1, 3)
    return shaped.reshape(row_tiles * col_tiles, TILE * TILE)

def from_tiles(tiled):
    shaped = tiled.reshape(D // TILE, KV // TILE, TILE, TILE).transpose(0, 2, 1, 3)
    return shaped.reshape(D, KV)

def reference(activations, cotangent, next_inputs, weight_tiles, momentum, chosen, counts):
    highest = lax.Precision.HIGHEST
    keep_rows = cosine_rows(KEEP)
    grad_scale = 1.0 / math.sqrt(ROWS_REP)
    act_groups = activations.reshape(REPLICAS, TOK_SHARDS, TOK_DEV, D)
    cot_groups = cotangent.reshape(REPLICAS, TOK_SHARDS, TOK_DEV, KV)
    slot_ids = jnp.arange(SLOTS, dtype=jnp.int32)
    offsets = (jnp.arange(TOK_SHARDS, dtype=jnp.int32) * TILES_DEV)[:, None]

    def one_replica(summed, replica_data):
        act_rep, cot_rep, moment_rep, chosen_rep, counts_rep = replica_data

        def add_shard(total, shard_data):
            product = jnp.dot(shard_data[0].T, shard_data[1], preferred_element_type=jnp.float32) * grad_scale
            rounded = lax.optimization_barrier(to_tiles(product).astype(jnp.bfloat16))
            return (total + rounded.astype(jnp.float32), None)
        gradient, _ = lax.scan(add_shard, jnp.zeros((TILES, TILE * TILE), jnp.float32), (act_rep, cot_rep))
        updated = momentum_decay * moment_rep + gradient
        global_ids = (offsets + chosen_rep).reshape(-1).astype(jnp.int32)
        in_list = (slot_ids[None, :] < counts_rep[:, None]).reshape(-1)
        picked = updated[global_ids].reshape(-1, TILE, TILE)
        quadrant = jnp.einsum('ua,nab,vb->nuv', keep_rows, picked, keep_rows, precision=highest)
        quadrant = lax.optimization_barrier(jnp.where(in_list[:, None, None], quadrant, 0.0).astype(jnp.bfloat16))
        quadrant = quadrant.astype(jnp.float32)
        rebuilt = jnp.einsum('ua,nuv,vb->nab', keep_rows, quadrant, keep_rows, precision=highest)
        residual = updated.at[global_ids].add(-rebuilt.reshape(-1, TILE * TILE))
        summed = summed.at[global_ids].add(quadrant.reshape(-1, KEEP * KEEP))
        return (summed, residual)
    summed, new_momentum = lax.scan(one_replica, jnp.zeros((TILES, KEEP * KEEP), jnp.float32), (act_groups, cot_groups, momentum, chosen, counts))
    update = jnp.einsum('ua,tuv,vb->tab', keep_rows, summed.reshape(TILES, KEEP, KEEP), keep_rows, precision=highest)
    new_tiles = (weight_tiles.astype(jnp.float32) - step_size * update.reshape(TILES, TILE * TILE)).astype(jnp.bfloat16)
    values = jnp.dot(next_inputs, from_tiles(new_tiles), preferred_element_type=jnp.float32).astype(jnp.bfloat16)
    return (values, new_momentum)
```

```python
import functools
import math

import jax
import jax.numpy as jnp
import numpy as np
from jax import lax
from jax.experimental import pallas as pl
from jax.experimental.pallas import tpu as pltpu
from jax.sharding import PartitionSpec as P

TILE = 64
KEEP = 32
LANES = 128


momentum_decay = 0.9
step_size = 0.01

HIGHEST = lax.Precision.HIGHEST


def cosine_rows(count):
    frequency = jnp.arange(count, dtype=jnp.float32)[:, None]
    position = jnp.arange(TILE, dtype=jnp.float32)[None, :]
    cosines = jnp.cos(math.pi * (2.0 * position + 1.0) * frequency / (2.0 * TILE))
    factor = jnp.where(frequency == 0, math.sqrt(1.0 / TILE), math.sqrt(2.0 / TILE))
    return cosines * factor


def rebuild(summed, weight_part, keep_rows):
    quads = summed.reshape(summed.shape[0], KEEP, KEEP)
    update = jnp.einsum("ua,tuv,vb->tab", keep_rows, quads, keep_rows, precision=HIGHEST)
    shifted = weight_part.astype(jnp.float32) - step_size * update.reshape(
        summed.shape[0], TILE * TILE
    )
    return shifted.astype(jnp.bfloat16)


def forward(inputs, new_tiles):
    row_tiles = inputs.shape[1] // TILE
    col_tiles = new_tiles.shape[0] // row_tiles
    blocks = inputs.reshape(inputs.shape[0], row_tiles, TILE)
    matrix = new_tiles.reshape(row_tiles, col_tiles, TILE, TILE)
    output = jnp.einsum("tra,rcab->tcb", blocks, matrix, preferred_element_type=jnp.float32)
    return output.reshape(inputs.shape[0], col_tiles * TILE).astype(jnp.bfloat16)


def general(activations, cotangent, next_inputs, weight_tiles, momentum, chosen, counts):
    shards = lax.axis_size("tok")
    tiles_here = weight_tiles.shape[0]
    row_tiles = activations.shape[1] // TILE
    col_tiles = cotangent.shape[1] // TILE
    grad_scale = 1.0 / math.sqrt(activations.shape[0] * shards)
    keep_rows = cosine_rows(KEEP)
    product = (
        lax.dot_general(
            activations, cotangent, (((0,), (0,)), ((), ())), preferred_element_type=jnp.float32
        )
        * grad_scale
    )
    tiled = product.reshape(row_tiles, TILE, col_tiles, TILE).transpose(0, 2, 1, 3)
    tiled = tiled.reshape(row_tiles * col_tiles, TILE * TILE)
    gradient = lax.psum_scatter(
        tiled.astype(jnp.bfloat16), "tok", scatter_dimension=0, tiled=True
    ).astype(jnp.float32)
    updated = momentum_decay * momentum[0] + gradient
    chosen_here = chosen[0, 0]
    in_list = jnp.arange(chosen_here.shape[0], dtype=jnp.int32) < counts[0, 0]
    picked = jnp.take(updated, chosen_here, axis=0).reshape(-1, TILE, TILE)
    quadrant = jnp.einsum("ua,nab,vb->nuv", keep_rows, picked, keep_rows, precision=HIGHEST)
    quadrant = jnp.where(in_list[:, None, None], quadrant, 0.0).astype(jnp.bfloat16)
    rebuilt = jnp.einsum(
        "ua,nuv,vb->nab", keep_rows, quadrant.astype(jnp.float32), keep_rows, precision=HIGHEST
    )
    new_momentum = updated.at[chosen_here].add(-rebuilt.reshape(-1, TILE * TILE))
    listed = jnp.where(in_list, chosen_here, -1)
    flat_quads = quadrant.reshape(-1, KEEP * KEEP)
    tile_numbers = jnp.arange(tiles_here, dtype=jnp.int32)
    all_quads, all_listed = (
        lax.all_gather(flat_quads, "replica", axis=0, tiled=True),
        lax.all_gather(listed, "replica", axis=0, tiled=True),
    )
    one_hot = (all_listed[:, None] == tile_numbers[None, :]).astype(jnp.bfloat16)
    summed = lax.dot_general(
        one_hot, all_quads, (((0,), (0,)), ((), ())), preferred_element_type=jnp.float32
    )
    new_part = rebuild(summed, weight_tiles, keep_rows)
    new_full = lax.all_gather(new_part, "tok", axis=0, tiled=True)
    values = forward(next_inputs, new_full)
    return (values, new_momentum[None])


def low_rows():
    u = np.arange(KEEP)[:, None].astype(np.float64)
    i = np.arange(TILE)[None, :].astype(np.float64)
    factor = np.where(u == 0, math.sqrt(1.0 / TILE), math.sqrt(2.0 / TILE))
    return np.cos(math.pi * (2 * i + 1) * u / (2 * TILE)) * factor


def tables():
    low = low_rows()
    split = np.concatenate([low[:, 0::2], low[:, 1::2]], axis=0)
    into = np.zeros((4 * LANES, LANES))
    back = np.zeros((LANES, 4 * LANES))
    for g in range(4):
        into[g * LANES : g * LANES + TILE, g * KEEP : (g + 1) * KEEP] = low.T
        for half in range(2):
            at = g * LANES + half * TILE
            back[g * KEEP : (g + 1) * KEEP, at : at + TILE] = low
    split_back = np.concatenate([low[:, 0::2].T, low[:, 1::2].T], axis=0)
    return [t.astype(np.float32) for t in (split, into, split_back, back)]


def lane_index(shape):
    return lax.broadcasted_iota(jnp.int32, shape, len(shape) - 1)


def tile_products(start, act_ref, cot_ref, sent_ref, cot_row, grid_ref, tiled_ref, scale, spans):
    tokens = act_ref.shape[1]
    width = cot_ref.shape[1]
    first_half = lane_index((KEEP, LANES)) < TILE
    step = 2 * TILE
    theirs = [
        sent_ref[0][cot_row + n * tokens : cot_row + (n + 1) * tokens, :]
        for n in range(width // tokens)
    ]
    for block in range(spans // 2):
        rows = pl.ds(pl.multiple_of(start + block * step, TILE), step)
        mine = jnp.dot(act_ref[rows, :], cot_ref[...], preferred_element_type=jnp.float32)
        other = sent_ref[1][block * step : (block + 1) * step, :]
        for n, piece in enumerate(theirs):
            lanes = slice(n * tokens, (n + 1) * tokens)
            theirs_here = jnp.dot(other, piece, preferred_element_type=jnp.float32)
            both = (mine[:, lanes] + theirs_here) * scale
            for m in range(tokens // LANES):
                grid_ref[n * (tokens // LANES) + m] = both[:, m * LANES : (m + 1) * LANES]
        for half in range(2):
            for m in range(width // LANES):
                even = grid_ref[m, pl.ds(half * TILE, KEEP, stride=2), :]
                odd = grid_ref[m, pl.ds(half * TILE + 1, KEEP, stride=2), :]
                tile = (2 * block + half) * (width // TILE) + 2 * m
                tiled_ref[tile * KEEP : (tile + 1) * KEEP, :] = jnp.where(
                    first_half, even, pltpu.roll(odd, TILE, 1)
                )
                tiled_ref[(tile + 1) * KEEP : (tile + 2) * KEEP, :] = jnp.where(
                    first_half, pltpu.roll(even, TILE, 1), odd
                )


def to_low(picked, split_ref, into_ref):
    wide = jnp.concatenate(picked, axis=1)
    mixed = jnp.dot(split_ref[...], wide, precision=HIGHEST, preferred_element_type=jnp.float32)
    out = []
    for h in range(len(picked) // 4):
        pieces = []
        for g in range(4):
            lanes = slice((4 * h + g) * LANES, (4 * h + g + 1) * LANES)
            pieces.append(mixed[:KEEP, lanes] + pltpu.roll(mixed[KEEP:, lanes], TILE, 1))
        row = jnp.concatenate(pieces, axis=1)
        out.append(
            jnp.dot(row, into_ref[...], precision=HIGHEST, preferred_element_type=jnp.float32)
        )
    return out


def far_kernel(
    at_ref, chosen_ref, act_ref, cot_ref, sent_ref, split_ref, into_ref,
    sum_ref, low_ref, grid_ref, tiled_ref, *, scale, spans,
):
    start, skip = at_ref[0], at_ref[1]
    tile_products(
        start, act_ref, cot_ref, (sent_ref, sent_ref), spans * TILE, grid_ref, tiled_ref, scale,
        spans,
    )
    slots = chosen_ref.shape[0]
    picked = [
        tiled_ref[pl.ds(pl.multiple_of((skip + chosen_ref[s]) * KEEP, KEEP), KEEP), :]
        for s in range(slots)
    ]
    for h, part in enumerate(to_low(picked, split_ref, into_ref)):
        low_ref[h * KEEP : (h + 1) * KEEP, :] = part
    rows = sum_ref.shape[0]
    chunk = 10 * KEEP
    for c in range(0, rows, chunk):
        sum_ref[c : c + chunk, :] = tiled_ref[
            pl.ds(pl.multiple_of(skip * KEEP + c, KEEP), chunk), :
        ].astype(jnp.bfloat16)


def own_kernel(
    at_ref, chosen_ref, act_ref, cot_ref, sent_ref, near_ref, mom_ref, far_low_ref,
    split_ref, into_ref, split_back_ref, back_ref,
    base_ref, quad_ref, grid_ref, tiled_ref, *, scale, spans,
):
    start, skip, count = at_ref[0], at_ref[1], at_ref[2]
    tile_products(
        start, act_ref, cot_ref, (sent_ref, near_ref), spans * TILE, grid_ref, tiled_ref, scale,
        spans,
    )
    rows = base_ref.shape[0]
    chunk = 10 * KEEP
    for c in range(0, rows, chunk):
        base_ref[c : c + chunk, :] = (
            momentum_decay * mom_ref[c : c + chunk, :]
            + tiled_ref[pl.ds(pl.multiple_of(skip * KEEP + c, KEEP), chunk), :]
        )
    slots = chosen_ref.shape[0]
    places = [
        pl.ds(pl.multiple_of(chosen_ref[s] * KEEP, KEEP), KEEP) for s in range(slots)
    ]
    lows = to_low([base_ref[place, :] for place in places], split_ref, into_ref)
    group = lane_index((KEEP, LANES)) // KEEP
    first_half = lax.rem(lane_index((KEEP, 4 * LANES)), LANES) < TILE
    for h, low in enumerate(lows):
        low = low + far_low_ref[h * KEEP : (h + 1) * KEEP, :]
        quad = jnp.where(group + 4 * h < count, low, 0.0).astype(jnp.bfloat16)
        quad_ref[h * KEEP : (h + 1) * KEEP, :] = quad
        wide = jnp.dot(
            quad.astype(jnp.float32), back_ref[...], precision=HIGHEST,
            preferred_element_type=jnp.float32,
        )
        both = jnp.dot(
            split_back_ref[...], wide, precision=HIGHEST, preferred_element_type=jnp.float32
        )
        rebuilt = jnp.where(first_half, both[:KEEP, :], both[KEEP:, :])
        for g in range(4):
            place = places[4 * h + g]
            base_ref[place, :] = base_ref[place, :] - rebuilt[:, g * LANES : (g + 1) * LANES]


def lows_kernel(inputs_ref, high_ref, low_ref, out_ref, lows_ref, *, span):
    rows = inputs_ref.shape[0]
    half = span // 2
    lows_ref[...] = jnp.zeros_like(lows_ref)
    for c in range(rows // span):
        piece = inputs_ref[c * span : (c + 1) * span, :]
        lows_ref[c * half : (c + 1) * half, :] = jnp.dot(
            high_ref[...], piece, preferred_element_type=jnp.float32
        ) + jnp.dot(low_ref[...], piece, preferred_element_type=jnp.float32)
    out_ref[...] = lows_ref[...].T.astype(jnp.bfloat16)


def last_kernel(tiles_ref, quads_ref, lows_ref, base_ref, high_ref, low_ref, out_ref, sum_ref,
                *, slots, col_tiles):
    sum_ref[...] = jnp.zeros_like(sum_ref)
    group = lane_index((KEEP, LANES)) // KEEP
    held = (slots // 4) * KEEP

    def add_list(n, carry):
        puts = []
        for s in range(slots):
            tile = tiles_ref[n * slots + s]
            i, j = tile // col_tiles, lax.rem(tile, col_tiles)
            h, g = s // 4, s % 4
            at = pl.ds(pl.multiple_of(n * held + h * KEEP, KEEP), KEEP)
            quad = quads_ref[at, :].astype(jnp.float32)
            to = lax.rem(j, 4)
            moved = pltpu.roll(quad, lax.rem(to - g + 4, 4) * KEEP, 1)
            place = sum_ref.at[j // 4, pl.ds(pl.multiple_of(i * KEEP, KEEP), KEEP)]
            puts.append((place, place[...] + moved, group == to))
        for place, value, mask in puts:
            pltpu.store(place, value, mask=mask)
        return carry

    lax.fori_loop(0, quads_ref.shape[0] // held, add_list, 0)
    parts = []
    for half in range(sum_ref.shape[0]):
        whole = sum_ref[half]
        top = whole.astype(jnp.bfloat16)
        rest = (whole - top.astype(jnp.float32)).astype(jnp.bfloat16)
        parts.append(
            jnp.dot(lows_ref[...], top, preferred_element_type=jnp.float32)
            + jnp.dot(lows_ref[...], rest, preferred_element_type=jnp.float32)
        )
    mixed = jnp.concatenate(parts, axis=1)
    top = mixed.astype(jnp.bfloat16)
    rest = (mixed - top.astype(jnp.float32)).astype(jnp.bfloat16)
    update = (
        jnp.dot(top, high_ref[...], preferred_element_type=jnp.float32)
        + jnp.dot(rest, high_ref[...], preferred_element_type=jnp.float32)
        + jnp.dot(top, low_ref[...], preferred_element_type=jnp.float32)
    )
    out_ref[...] = (base_ref[...] - step_size * update).astype(jnp.bfloat16)


def split_bf16(table):
    top = table.astype(jnp.bfloat16)
    return top, (table - top.astype(np.float32)).astype(jnp.bfloat16)


def vmem(count):
    return [pl.BlockSpec(memory_space=pltpu.VMEM)] * count


def smem(count):
    return [pl.BlockSpec(memory_space=pltpu.SMEM)] * count


def swap(array, axis, bit):
    size = lax.axis_size(axis)
    return lax.ppermute(array, axis, [(i, i ^ bit) for i in range(size)])


def doubled(array, axis, bit):
    return jnp.concatenate([array, swap(array, axis, bit)], axis=0)


def fits(shards, replicas, activations, cotangent, weight_tiles, slots):
    tokens, depth = activations.shape
    width = cotangent.shape[1]
    tiles_here = weight_tiles.shape[0]
    span = span_of(tiles_here, width // TILE)
    return (
        shards == 4
        and replicas == 8
        and tokens % LANES == 0
        and width % tokens == 0
        and width // TILE == 8
        and slots % 4 == 0
        and depth % (5 * TILE) == 0
        and tiles_here % 10 == 0
        and tiles_here <= 256
        and slots <= 128
        and span % 2 == 0
        and all((n * tiles_here) // 8 + span <= depth // TILE for n in range(shards))
        and all((n * tiles_here) % 8 + tiles_here <= span * 8 for n in range(shards))
    )


def span_of(tiles_here, col_tiles):
    return 2 * (-(-tiles_here // col_tiles) // 2)


def local(activations, cotangent, next_inputs, weight_tiles, momentum, chosen, counts):
    shards = lax.axis_size("tok")
    replicas = lax.axis_size("replica")
    slots = chosen.shape[-1]
    if not fits(shards, replicas, activations, cotangent, weight_tiles, slots):
        return general(
            activations, cotangent, next_inputs, weight_tiles, momentum, chosen, counts
        )
    tokens, depth = activations.shape
    width = cotangent.shape[1]
    tiles_here = weight_tiles.shape[0]
    row_tiles = depth // TILE
    col_tiles = width // TILE
    spans = span_of(tiles_here, col_tiles)
    span_rows = spans * TILE
    scale = 1.0 / math.sqrt(tokens * shards)
    me = lax.axis_index("tok")
    rep = lax.axis_index("replica")
    act = activations.T
    inputs = next_inputs.T
    split, into, split_back, back = tables()

    def start_of(shard):
        return (shard * tiles_here) // col_tiles * TILE

    def skip_of(shard):
        return lax.rem(shard * tiles_here, col_tiles)

    def rows_for(shard):
        return lax.dynamic_slice(act, (start_of(shard), 0), (span_rows, tokens))

    share = TILE * TILE // replicas
    listed = chosen[0, 0].astype(jnp.bfloat16)
    pad_rows = -(tiles_here + 1) % 8 + 1
    piece = jnp.concatenate(
        [
            lax.dynamic_slice(weight_tiles, (0, rep * share), (tiles_here, share)),
            jnp.zeros((pad_rows, share), jnp.bfloat16).at[0, :slots].set(listed),
        ],
        axis=0,
    )[None]

    cot_parts = [cotangent[:, n * tokens : (n + 1) * tokens] for n in range(width // tokens)]
    sent_far = swap(jnp.concatenate([rows_for(me ^ 3), *cot_parts], axis=0), "tok", 1)
    pieces = doubled(doubled(piece, "tok", 1), "tok", 2)
    sent_near = swap(rows_for(me ^ 1), "tok", 1)

    lists = pieces[:, tiles_here, :slots]
    far = me ^ 2
    far_chosen = lists[2].astype(jnp.int32)
    grid_scratch = [
        pltpu.VMEM((width // LANES, 2 * TILE, LANES), jnp.float32),
        pltpu.VMEM((spans * col_tiles * KEEP, LANES), jnp.float32),
    ]
    far_sum, far_low = pl.pallas_call(
        functools.partial(far_kernel, scale=scale, spans=spans),
        out_shape=(
            jax.ShapeDtypeStruct((tiles_here * KEEP, LANES), jnp.bfloat16),
            jax.ShapeDtypeStruct((slots // 4 * KEEP, LANES), jnp.float32),
        ),
        in_specs=smem(2) + vmem(5),
        out_specs=tuple(vmem(2)),
        scratch_shapes=grid_scratch,
        name="far",
    )(
        jnp.stack([start_of(far), skip_of(far)]), far_chosen, act, cotangent, sent_far,
        split, into,
    )
    low_from = swap(far_low, "tok", 2)
    sum_from = swap(far_sum, "tok", 2)

    moment = momentum.reshape(tiles_here * KEEP, LANES)
    base, quads = pl.pallas_call(
        functools.partial(own_kernel, scale=scale, spans=spans),
        out_shape=(
            jax.ShapeDtypeStruct((tiles_here * KEEP, LANES), jnp.float32),
            jax.ShapeDtypeStruct((slots // 4 * KEEP, LANES), jnp.bfloat16),
        ),
        in_specs=smem(2) + vmem(10),
        out_specs=tuple(vmem(2)),
        scratch_shapes=grid_scratch,
        name="own",
    )(
        jnp.stack([start_of(me), skip_of(me), counts[0, 0]]), chosen[0, 0], act, cotangent,
        sent_far, sent_near, moment, low_from, split, into, split_back, back,
    )
    new_momentum = (base + sum_from.astype(jnp.float32)).reshape(momentum.shape)

    shard_order = [lax.dynamic_index_in_dim(pieces, me ^ n, 0, False) for n in range(shards)]
    whole = jnp.concatenate([p[:tiles_here] for p in shard_order], axis=0)
    rows_share = TILE // replicas
    matrix = whole.reshape(row_tiles, col_tiles, rows_share, TILE).transpose(0, 2, 1, 3)
    matrix = matrix.reshape(row_tiles * rows_share, width)
    list_rows = jnp.zeros((8, width), jnp.bfloat16).at[:shards, :slots].set(lists)
    held = jnp.concatenate([matrix, list_rows], axis=0)[None]
    for bit in (2, 4, 1):
        held = doubled(held, "replica", bit)
    all_lists = held[:, matrix.shape[0] : matrix.shape[0] + shards, :slots].astype(jnp.int32)
    owners = me ^ jnp.arange(shards, dtype=jnp.int32)
    all_tiles = (all_lists + (owners * tiles_here)[None, :, None]).reshape(-1)
    order = [n1 * 1 ^ n2 * 4 ^ n3 * 2 for n1 in range(2) for n2 in range(2) for n3 in range(2)]
    by_share = inputs.reshape(row_tiles, replicas, rows_share, tokens)
    mine = jnp.concatenate(
        [
            lax.dynamic_index_in_dim(by_share, rep ^ o, 1, False).reshape(-1, tokens)
            for o in order
        ],
        axis=0,
    )
    kept = held[:, : matrix.shape[0]].reshape(depth, width)
    unchanged = lax.dot_general(
        mine, kept, (((0,), (0,)), ((), ())), preferred_element_type=jnp.float32
    )

    low = low_rows().astype(np.float32)
    at_once = 5
    along = np.kron(np.eye(at_once, dtype=np.float32), low)
    along_high, along_low = split_bf16(along)
    padded = -(-row_tiles * KEEP // LANES) * LANES
    lows = pl.pallas_call(
        functools.partial(lows_kernel, span=at_once * TILE),
        out_shape=jax.ShapeDtypeStruct((tokens, padded), jnp.bfloat16),
        in_specs=vmem(3),
        out_specs=vmem(1)[0],
        scratch_shapes=[pltpu.VMEM((padded, tokens), jnp.float32)],
        name="lows",
    )(inputs, along_high, along_low)

    gathered = doubled(doubled(quads[None], "tok", 1), "tok", 2)
    for bit in (2, 4, 1):
        gathered = doubled(gathered, "replica", bit)
    across = np.kron(np.eye(col_tiles, dtype=np.float32), low)
    across_high, across_low = split_bf16(across)
    values = pl.pallas_call(
        functools.partial(last_kernel, slots=slots, col_tiles=col_tiles),
        out_shape=jax.ShapeDtypeStruct((tokens, width), jnp.bfloat16),
        in_specs=smem(1) + vmem(5),
        out_specs=vmem(1)[0],
        scratch_shapes=[pltpu.VMEM((col_tiles // 4, padded, LANES), jnp.float32)],
        name="last",
    )(all_tiles, gathered.reshape(-1, LANES), lows, unchanged, across_high, across_low)
    return (values, new_momentum)


def solution(mesh):
    return jax.shard_map(
        local,
        mesh=mesh,
        in_specs=(
            P(("replica", "tok"), None),
            P(("replica", "tok"), None),
            P(("replica", "tok"), None),
            P("tok", None),
            P("replica", "tok", None),
            P("replica", "tok", None),
            P("replica", "tok"),
        ),
        out_specs=(P(("replica", "tok"), None), P("replica", "tok", None)),
        check_vma=False,
    )
```

```python
import functools
import math

import jax
import jax.numpy as jnp
import numpy as np
from jax import lax
from jax.experimental import pallas as pl
from jax.experimental.pallas import tpu as pltpu
from jax.sharding import PartitionSpec as P


TILE = 64
KEEP = 32
LANES = 128


momentum_decay = 0.9
step_size = 0.01

HIGHEST = lax.Precision.HIGHEST

TOK_ORDER = (0, 2, 1, 3)
SHARE_ORDER = (0, 2, 4, 1, 3, 5, 6, 7)
HELD_ORDER = (0, 2, 4, 6, 6, 1, 3, 5, 7, 7)


def cosine_rows(count):
    frequency = jnp.arange(count, dtype=jnp.float32)[:, None]
    position = jnp.arange(TILE, dtype=jnp.float32)[None, :]
    cosines = jnp.cos(math.pi * (2.0 * position + 1.0) * frequency / (2.0 * TILE))
    factor = jnp.where(frequency == 0, math.sqrt(1.0 / TILE), math.sqrt(2.0 / TILE))
    return cosines * factor


def rebuild(summed, weight_part, keep_rows):
    quads = summed.reshape(summed.shape[0], KEEP, KEEP)
    update = jnp.einsum("ua,tuv,vb->tab", keep_rows, quads, keep_rows, precision=HIGHEST)
    shifted = weight_part.astype(jnp.float32) - step_size * update.reshape(
        summed.shape[0], TILE * TILE
    )
    return shifted.astype(jnp.bfloat16)


def forward(inputs, new_tiles):
    row_tiles = inputs.shape[1] // TILE
    col_tiles = new_tiles.shape[0] // row_tiles
    blocks = inputs.reshape(inputs.shape[0], row_tiles, TILE)
    matrix = new_tiles.reshape(row_tiles, col_tiles, TILE, TILE)
    output = jnp.einsum("tra,rcab->tcb", blocks, matrix, preferred_element_type=jnp.float32)
    return output.reshape(inputs.shape[0], col_tiles * TILE).astype(jnp.bfloat16)


def general(activations, cotangent, next_inputs, weight_tiles, momentum, chosen, counts):
    shards = lax.axis_size("tok")
    tiles_here = weight_tiles.shape[0]
    row_tiles = activations.shape[1] // TILE
    col_tiles = cotangent.shape[1] // TILE
    grad_scale = 1.0 / math.sqrt(activations.shape[0] * shards)
    keep_rows = cosine_rows(KEEP)
    product = (
        lax.dot_general(
            activations, cotangent, (((0,), (0,)), ((), ())), preferred_element_type=jnp.float32
        )
        * grad_scale
    )
    tiled = product.reshape(row_tiles, TILE, col_tiles, TILE).transpose(0, 2, 1, 3)
    tiled = tiled.reshape(row_tiles * col_tiles, TILE * TILE)
    gradient = lax.psum_scatter(
        tiled.astype(jnp.bfloat16), "tok", scatter_dimension=0, tiled=True
    ).astype(jnp.float32)
    updated = momentum_decay * momentum[0] + gradient
    chosen_here = chosen[0, 0]
    in_list = jnp.arange(chosen_here.shape[0], dtype=jnp.int32) < counts[0, 0]
    picked = jnp.take(updated, chosen_here, axis=0).reshape(-1, TILE, TILE)
    quadrant = jnp.einsum("ua,nab,vb->nuv", keep_rows, picked, keep_rows, precision=HIGHEST)
    quadrant = jnp.where(in_list[:, None, None], quadrant, 0.0).astype(jnp.bfloat16)
    rebuilt = jnp.einsum(
        "ua,nuv,vb->nab", keep_rows, quadrant.astype(jnp.float32), keep_rows, precision=HIGHEST
    )
    new_momentum = updated.at[chosen_here].add(-rebuilt.reshape(-1, TILE * TILE))
    listed = jnp.where(in_list, chosen_here, -1)
    flat_quads = quadrant.reshape(-1, KEEP * KEEP)
    tile_numbers = jnp.arange(tiles_here, dtype=jnp.int32)
    all_quads, all_listed = (
        lax.all_gather(flat_quads, "replica", axis=0, tiled=True),
        lax.all_gather(listed, "replica", axis=0, tiled=True),
    )
    one_hot = (all_listed[:, None] == tile_numbers[None, :]).astype(jnp.bfloat16)
    summed = lax.dot_general(
        one_hot, all_quads, (((0,), (0,)), ((), ())), preferred_element_type=jnp.float32
    )
    new_part = rebuild(summed, weight_tiles, keep_rows)
    new_full = lax.all_gather(new_part, "tok", axis=0, tiled=True)
    values = forward(next_inputs, new_full)
    return (values, new_momentum[None])


def low_rows():
    u = np.arange(KEEP)[:, None].astype(np.float64)
    i = np.arange(TILE)[None, :].astype(np.float64)
    factor = np.where(u == 0, math.sqrt(1.0 / TILE), math.sqrt(2.0 / TILE))
    return np.cos(math.pi * (2 * i + 1) * u / (2 * TILE)) * factor


def tables():
    low = low_rows()
    split = np.concatenate([low[:, 0::2], low[:, 1::2]], axis=0)
    into = np.zeros((4 * LANES, LANES))
    back = np.zeros((LANES, 4 * LANES))
    for g in range(4):
        into[g * LANES : g * LANES + TILE, g * KEEP : (g + 1) * KEEP] = low.T
        for half in range(2):
            at = g * LANES + half * TILE
            back[g * KEEP : (g + 1) * KEEP, at : at + TILE] = low
    split_back = np.concatenate([low[:, 0::2].T, low[:, 1::2].T], axis=0)
    return [t.astype(np.float32) for t in (split, into, split_back, back)]


def lane_index(shape):
    return lax.broadcasted_iota(jnp.int32, shape, len(shape) - 1)


def tile_products(act_ref, cot_ref, sent_ref, cot_row, grid_ref, tiled_ref, scale, spans):
    tokens = act_ref.shape[1]
    width = cot_ref.shape[1]
    first_half = lane_index((KEEP, LANES)) < TILE
    step = 2 * TILE
    theirs = [
        sent_ref[0][cot_row + n * tokens : cot_row + (n + 1) * tokens, :]
        for n in range(width // tokens)
    ]
    for block in range(spans // 2):
        rows = slice(block * step, (block + 1) * step)
        mine = jnp.dot(act_ref[rows, :], cot_ref[...], preferred_element_type=jnp.float32)
        other = sent_ref[1][rows, :]
        for n, piece in enumerate(theirs):
            lanes = slice(n * tokens, (n + 1) * tokens)
            theirs_here = jnp.dot(other, piece, preferred_element_type=jnp.float32)
            both = (mine[:, lanes] + theirs_here) * scale
            for m in range(tokens // LANES):
                grid_ref[n * (tokens // LANES) + m] = both[:, m * LANES : (m + 1) * LANES]
        for half in range(2):
            for m in range(width // LANES):
                even = grid_ref[m, pl.ds(half * TILE, KEEP, stride=2), :]
                odd = grid_ref[m, pl.ds(half * TILE + 1, KEEP, stride=2), :]
                tile = (2 * block + half) * (width // TILE) + 2 * m
                tiled_ref[tile * KEEP : (tile + 1) * KEEP, :] = jnp.where(
                    first_half, even, pltpu.roll(odd, TILE, 1)
                )
                tiled_ref[(tile + 1) * KEEP : (tile + 2) * KEEP, :] = jnp.where(
                    first_half, pltpu.roll(even, TILE, 1), odd
                )


def to_low(picked, split_ref, into_ref):
    wide = jnp.concatenate(picked, axis=1)
    mixed = jnp.dot(split_ref[...], wide, preferred_element_type=jnp.float32)
    out = []
    for h in range(len(picked) // 4):
        pieces = []
        for g in range(4):
            lanes = slice((4 * h + g) * LANES, (4 * h + g + 1) * LANES)
            pieces.append(mixed[:KEEP, lanes] + pltpu.roll(mixed[KEEP:, lanes], TILE, 1))
        row = jnp.concatenate(pieces, axis=1)
        out.append(jnp.dot(row, into_ref[...], preferred_element_type=jnp.float32))
    return out


def far_kernel(
    chosen_ref, act_ref, cot_ref, sent_ref, split_ref, into_ref,
    low_ref, *rest, scale, spans, tiles_here,
):
    sum_refs, (grid_ref, tiled_ref) = rest[:-2], rest[-2:]
    skip = first_skip(lax.axis_index("tok") ^ 2, tiles_here, cot_ref.shape[1] // TILE)
    tile_products(
        act_ref, cot_ref, (sent_ref, sent_ref), spans * TILE, grid_ref, tiled_ref, scale, spans
    )
    slots = chosen_ref.shape[0]
    picked = [
        tiled_ref[pl.ds(pl.multiple_of((skip + chosen_ref[s]) * KEEP, KEEP), KEEP), :]
        for s in range(slots)
    ]
    for h, part in enumerate(to_low(picked, split_ref, into_ref)):
        low_ref[h * KEEP : (h + 1) * KEEP, :] = part
    first = 0
    for sum_ref in sum_refs:
        rows = sum_ref.shape[0]
        for c in range(0, rows, 2 * KEEP):
            n = min(2 * KEEP, rows - c)
            sum_ref[c : c + n, :] = tiled_ref[
                pl.ds(pl.multiple_of(skip * KEEP + first + c, KEEP), n), :
            ].astype(jnp.bfloat16)
        first += rows


def own_kernel(
    count_ref, chosen_ref, act_ref, cot_ref, sent_ref, near_ref, mom_ref, far_low_ref,
    split_ref, into_ref, split_back_ref, back_ref,
    part_ref, quad_ref, grid_ref, tiled_ref, held_ref, sems, *, scale, spans, tiles_here,
):
    skip = first_skip(lax.axis_index("tok"), tiles_here, cot_ref.shape[1] // TILE)
    count = count_ref[0]
    slots = chosen_ref.shape[0]
    copies = [
        pltpu.make_async_copy(
            mom_ref.at[pl.ds(pl.multiple_of(chosen_ref[s] * KEEP, KEEP), KEEP)],
            held_ref.at[s], sems.at[s],
        )
        for s in range(slots)
    ]
    for copy in copies:
        copy.start()
    tile_products(
        act_ref, cot_ref, (sent_ref, near_ref), spans * TILE, grid_ref, tiled_ref, scale, spans
    )
    for copy in copies:
        copy.wait()
    places = [
        pl.ds(pl.multiple_of((skip + chosen_ref[s]) * KEEP, KEEP), KEEP) for s in range(slots)
    ]
    picked = [momentum_decay * held_ref[s] + tiled_ref[places[s], :] for s in range(slots)]
    lows = to_low(picked, split_ref, into_ref)
    group = lane_index((KEEP, LANES)) // KEEP
    first_half = lax.rem(lane_index((KEEP, 4 * LANES)), LANES) < TILE
    for h, low in enumerate(lows):
        low = low + far_low_ref[h * KEEP : (h + 1) * KEEP, :]
        quad = jnp.where(group + 4 * h < count, low, 0.0).astype(jnp.bfloat16)
        quad_ref[h * KEEP : (h + 1) * KEEP, :] = quad
        wide = jnp.dot(
            quad.astype(jnp.float32), back_ref[...], preferred_element_type=jnp.float32
        )
        both = jnp.dot(split_back_ref[...], wide, preferred_element_type=jnp.float32)
        rebuilt = jnp.where(first_half, both[:KEEP, :], both[KEEP:, :])
        for g in range(4):
            place = places[4 * h + g]
            tiled_ref[place, :] = tiled_ref[place, :] - rebuilt[:, g * LANES : (g + 1) * LANES]
    rows = part_ref.shape[0]
    for c in range(0, rows, 2 * KEEP):
        part_ref[c : c + 2 * KEEP, :] = tiled_ref[
            pl.ds(pl.multiple_of(skip * KEEP + c, KEEP), 2 * KEEP), :
        ].astype(jnp.bfloat16)


def first_row(shard, tiles_here, col_tiles):
    return pl.multiple_of((shard * tiles_here) // col_tiles * TILE, TILE)


def first_skip(shard, tiles_here, col_tiles):
    return lax.rem(shard * tiles_here, col_tiles)


def run_copies(pairs, sems):
    copies = [pltpu.make_async_copy(a, b, sems.at[n]) for n, (a, b) in enumerate(pairs)]
    for copy in copies:
        copy.start()
    for copy in copies:
        copy.wait()


def prepare_kernel(act_ref, cot_ref, far_ref, near_ref, sems, *, tiles_here):
    rows, tokens = near_ref.shape
    me = lax.axis_index("tok")
    pick = lambda n: act_ref.at[pl.ds(first_row(me ^ n, tiles_here, cot_ref.shape[1] // TILE), rows)]
    pairs = [(pick(3), far_ref.at[pl.ds(0, rows)]), (pick(1), near_ref)]
    for n in range(cot_ref.shape[1] // tokens):
        lanes, at = pl.ds(n * tokens, tokens), pl.ds(rows + n * tokens, tokens)
        pairs.append((cot_ref.at[:, lanes], far_ref.at[at]))
    run_copies(pairs, sems)


def mine_kernel(act_ref, far_ref, near_ref, sems, *, tiles_here, col_tiles):
    rows = near_ref.shape[0]
    me = lax.axis_index("tok")
    pick = lambda n: act_ref.at[pl.ds(first_row(me ^ n, tiles_here, col_tiles), rows)]
    run_copies([(pick(2), far_ref), (pick(0), near_ref)], sems)


def reorder_kernel(order_ref, from_ref, to_ref, sems):
    size = from_ref.shape[0]
    for n in range(size, to_ref.shape[1]):
        to_ref[:, n] = jnp.zeros_like(to_ref[:, n])
    run_copies(
        [
            (from_ref.at[:, order_ref[n]], to_ref.at[n, pl.ds(0, size)])
            for n in range(to_ref.shape[0])
        ],
        sems,
    )


def finish_kernel(mom_ref, part_ref, *refs):
    sums, out_ref = refs[:-1], refs[-1]
    first = 0
    for ref in sums:
        for c in range(0, ref.shape[0], 2 * KEEP):
            n = min(2 * KEEP, ref.shape[0] - c)
            rows = slice(first + c, first + c + n)
            out_ref[rows, :] = (
                momentum_decay * mom_ref[rows, :]
                + part_ref[rows, :].astype(jnp.float32)
                + ref[c : c + n, :].astype(jnp.float32)
            )
        first += ref.shape[0]


def unchanged_kernel(mine_ref, *refs, tiles_here, list_row):
    held, (out_ref, place_ref) = refs[:-2], refs[-2:]
    size = held[0].shape[0]
    me = lax.axis_index("tok")
    lane = lane_index((1, LANES))
    slots_at = [(o, [r for r, k in zip(held, HELD_ORDER) if k == o]) for o in SHARE_ORDER]
    total = None
    for n, (_, pieces) in enumerate(slots_at):
        first = n * size
        for piece in pieces:
            x = mine_ref[first : first + piece.shape[0], :]
            first += piece.shape[0]
            term = lax.dot_general(
                x, piece[...], (((0,), (0,)), ((), ())), preferred_element_type=jnp.float32
            )
            total = term if total is None else total + term
        piece = pieces[-1]
        at = list_row - (size - piece.shape[0])
        lists = piece[at : at + 8, :LANES].astype(jnp.float32).astype(jnp.int32)
        row = jnp.zeros((1, LANES), jnp.int32)
        for d, offset in enumerate(TOK_ORDER):
            tile = lists[d : d + 1, :] + (me ^ offset) * tiles_here
            i, j = lax.shift_right_logical(tile, 3), tile & 7
            packed = (lax.shift_right_logical(j, 2) * place_rows(mine_ref) + i * KEEP) * LANES
            packed = packed + (j & 3) * KEEP
            packed = pltpu.roll(packed, 8 * d, 1)
            row = jnp.where((lane >= 8 * d) & (lane < 8 * (d + 1)), packed, row)
        place_ref[n : n + 1, :] = row
    out_ref[...] = total


def place_rows(mine_ref):
    depth = mine_ref.shape[0] - 8 * len(SHARE_ORDER)
    return -(-(depth // TILE * KEEP) // LANES) * LANES


def lows_kernel(inputs_ref, high_ref, low_ref, out_ref, lows_ref, *, span):
    rows = inputs_ref.shape[0]
    half = span // 2
    lows_ref[...] = jnp.zeros_like(lows_ref)
    for c in range(rows // span):
        piece = inputs_ref[c * span : (c + 1) * span, :]
        lows_ref[c * half : (c + 1) * half, :] = jnp.dot(
            high_ref[...], piece, preferred_element_type=jnp.float32
        ) + jnp.dot(low_ref[...], piece, preferred_element_type=jnp.float32)
    out_ref[...] = lows_ref[...].T.astype(jnp.bfloat16)


def add_quads(place_ref, n, quads_ref, sum_ref):
    first_lane = lane_index((KEEP, LANES)) // KEEP * KEEP
    slots = quads_ref.shape[1] // KEEP * 4

    def add_list(d, carry):
        puts = []
        for s in range(slots):
            h, g = s // 4, s % 4
            quad = quads_ref[d, h * KEEP : (h + 1) * KEEP, :]
            packed = place_ref[n, d * slots + s]
            to = packed & (LANES - 1)
            moved = pltpu.roll(quad.astype(jnp.float32), (to - g * KEEP) & (LANES - 1), 1)
            row = pl.multiple_of(lax.shift_right_logical(packed, 7), KEEP)
            place = sum_ref.at[pl.ds(row, KEEP)]
            puts.append((place, place[...] + moved, first_lane == to))
        for place, value, mask in puts:
            pltpu.store(place, value, mask=mask)
        return carry

    lax.fori_loop(0, quads_ref.shape[0], add_list, 0)


def begin_kernel(place_ref, *refs, at):
    quads, sum_ref = refs[:-1], refs[-1]
    sum_ref[...] = jnp.zeros_like(sum_ref)
    for n, ref in zip(at, quads):
        add_quads(place_ref, n, ref, sum_ref)


def last_kernel(place_ref, lows_ref, base_ref, across_ref, begun_ref, *refs, at):
    quads, (out_ref, sum_ref) = refs[:-2], refs[-2:]
    sum_ref[...] = begun_ref[...]
    for n, ref in zip(at, quads):
        add_quads(place_ref, n, ref, sum_ref)
    rows = lows_ref.shape[1]
    whole = jnp.concatenate(
        [
            sum_ref[n * rows : (n + 1) * rows, :].astype(jnp.bfloat16)
            for n in range(sum_ref.shape[0] // rows)
        ],
        axis=1,
    )
    mixed = jnp.dot(lows_ref[...], whole, preferred_element_type=jnp.float32)
    update = jnp.dot(
        mixed.astype(jnp.bfloat16), across_ref[...], preferred_element_type=jnp.float32
    )
    out_ref[...] = (base_ref[...] - step_size * update).astype(jnp.bfloat16)


def split_bf16(table):
    top = table.astype(jnp.bfloat16)
    return top, (table - top.astype(np.float32)).astype(jnp.bfloat16)


def room(mib):
    return pltpu.CompilerParams(vmem_limit_bytes=mib * 1024 * 1024)


def vmem(count):
    return [pl.BlockSpec(memory_space=pltpu.VMEM)] * count


def smem(count):
    return [pl.BlockSpec(memory_space=pltpu.SMEM)] * count


def swap(array, axis, bit):
    size = lax.axis_size(axis)
    return lax.ppermute(array, axis, [(i, i ^ bit) for i in range(size)])


def fits(shards, replicas, activations, cotangent, weight_tiles, slots):
    tokens, depth = activations.shape
    width = cotangent.shape[1]
    tiles_here = weight_tiles.shape[0]
    span = span_of(tiles_here, width // TILE)
    return (
        shards == 4
        and replicas == 8
        and tokens % LANES == 0
        and width % tokens == 0
        and width // TILE == 8
        and slots == 8
        and depth % (5 * TILE) == 0
        and tiles_here % 10 == 0
        and tiles_here <= 256
        and slots <= 128
        and span % 2 == 0
        and all((n * tiles_here) // 8 + span <= depth // TILE for n in range(shards))
        and all((n * tiles_here) % 8 + tiles_here <= span * 8 for n in range(shards))
    )


def span_of(tiles_here, col_tiles):
    return 2 * (-(-tiles_here // col_tiles) // 2)


def local(activations, cotangent, next_inputs, weight_tiles, momentum, chosen, counts):
    shards = lax.axis_size("tok")
    replicas = lax.axis_size("replica")
    slots = chosen.shape[-1]
    if not fits(shards, replicas, activations, cotangent, weight_tiles, slots):
        return general(
            activations, cotangent, next_inputs, weight_tiles, momentum, chosen, counts
        )
    return four_shards(
        activations, cotangent, next_inputs, weight_tiles, momentum, chosen, counts
    )


def four_shards(activations, cotangent, next_inputs, weight_tiles, momentum, chosen, counts):
    shards = lax.axis_size("tok")
    replicas = lax.axis_size("replica")
    slots = chosen.shape[-1]
    tokens, depth = activations.shape
    width = cotangent.shape[1]
    tiles_here = weight_tiles.shape[0]
    row_tiles = depth // TILE
    col_tiles = width // TILE
    spans = span_of(tiles_here, col_tiles)
    span_rows = spans * TILE
    scale = 1.0 / math.sqrt(tokens * shards)
    me = lax.axis_index("tok")
    rep = lax.axis_index("replica")
    act = activations.T
    inputs = next_inputs.T
    split, into, split_back, back = tables()

    def place_of(offset):
        return (offset & 1) * 2 + lax.shift_right_logical(offset, 1)

    anywhere = pl.BlockSpec(memory_space=pltpu.HBM)
    span_shape = jax.ShapeDtypeStruct((span_rows, tokens), jnp.bfloat16)
    sent_rows, near_rows = pl.pallas_call(
        functools.partial(prepare_kernel, tiles_here=tiles_here),
        out_shape=[
            jax.ShapeDtypeStruct((span_rows + width, tokens), jnp.bfloat16), span_shape,
        ],
        in_specs=[anywhere] * 2,
        out_specs=vmem(2),
        scratch_shapes=[pltpu.SemaphoreType.DMA((2 + width // tokens,))],
        name="prepare",
    )(act, cotangent)
    sent_far = swap(sent_rows, "tok", 1)
    mine_far, mine_near = pl.pallas_call(
        functools.partial(mine_kernel, tiles_here=tiles_here, col_tiles=col_tiles),
        out_shape=[span_shape] * 2,
        in_specs=[anywhere],
        out_specs=vmem(2),
        scratch_shapes=[pltpu.SemaphoreType.DMA((2,))],
        name="mine",
    )(act)
    share = TILE * TILE // replicas
    listed = chosen[0, 0].astype(jnp.bfloat16)
    pad_rows = -(tiles_here + 1) % 8 + 1
    piece = jnp.concatenate(
        [
            lax.dynamic_slice(weight_tiles, (0, rep * share), (tiles_here, share)),
            jnp.zeros((pad_rows, share), jnp.bfloat16).at[0, :slots].set(listed),
        ],
        axis=0,
    )[None]
    piece_far = swap(piece, "tok", 2)
    pair = jnp.concatenate([piece, piece_far], axis=0)
    pieces = jnp.concatenate([pair, swap(pair, "tok", 1)], axis=0)
    sent_near = swap(near_rows, "tok", 1)
    far_chosen = piece_far[0, tiles_here, :slots].astype(jnp.int32)
    grid_scratch = [
        pltpu.VMEM((width // LANES, 2 * TILE, LANES), jnp.float32),
        pltpu.VMEM((spans * col_tiles * KEEP, LANES), jnp.float32),
    ]
    cuts = [tiles_here * 8 // 15, tiles_here // 9]
    cuts.append(tiles_here - sum(cuts))
    far_low, *far_sums = pl.pallas_call(
        functools.partial(far_kernel, scale=scale, spans=spans, tiles_here=tiles_here),
        out_shape=[jax.ShapeDtypeStruct((slots // 4 * KEEP, LANES), jnp.float32)]
        + [jax.ShapeDtypeStruct((n * KEEP, LANES), jnp.bfloat16) for n in cuts],
        in_specs=smem(1) + vmem(5),
        out_specs=vmem(1 + len(cuts)),
        scratch_shapes=grid_scratch,
        name="far",
    )(far_chosen, mine_far, cotangent, sent_far, split, into)
    low_from = swap(far_low, "tok", 2)
    sums_from = []
    for part in far_sums:
        sums_from.append(swap(part, "tok", 2))

    moment = momentum.reshape(tiles_here * KEEP, LANES)
    own_part, quads = pl.pallas_call(
        functools.partial(own_kernel, scale=scale, spans=spans, tiles_here=tiles_here),
        out_shape=(
            jax.ShapeDtypeStruct((tiles_here * KEEP, LANES), jnp.bfloat16),
            jax.ShapeDtypeStruct((slots // 4 * KEEP, LANES), jnp.bfloat16),
        ),
        in_specs=smem(2) + vmem(4) + [anywhere] + vmem(5),
        out_specs=tuple(vmem(2)),
        scratch_shapes=grid_scratch
        + [pltpu.VMEM((slots, KEEP, LANES), jnp.float32), pltpu.SemaphoreType.DMA((slots,))],
        name="own",
    )(
        counts[0], chosen[0, 0], mine_near, cotangent, sent_far, sent_near, moment, low_from,
        split, into, split_back, back,
    )
    new_momentum = pl.pallas_call(
        finish_kernel,
        out_shape=jax.ShapeDtypeStruct(moment.shape, jnp.float32),
        in_specs=vmem(2 + len(cuts)),
        out_specs=vmem(1)[0],
        name="finish",
    )(moment, own_part, *sums_from).reshape(momentum.shape)

    whole = jnp.concatenate(
        [
            lax.dynamic_index_in_dim(pieces, place_of(me ^ n), 0, False)[:tiles_here]
            for n in range(shards)
        ],
        axis=0,
    )
    rows_share = TILE // replicas
    matrix = whole.reshape(row_tiles, col_tiles, rows_share, TILE).transpose(0, 2, 1, 3)
    matrix = matrix.reshape(row_tiles * rows_share, width)
    list_rows = jnp.zeros((8, width), jnp.bfloat16)
    list_rows = list_rows.at[:shards, :slots].set(pieces[:, tiles_here, :slots])
    held = {0: jnp.concatenate([matrix, list_rows], axis=0)}
    cut = held[0].shape[0] // 2
    held[2] = swap(held[0], "replica", 2)
    held[4] = swap(held[0], "replica", 4)
    six = [swap(held[2][:cut], "replica", 4)]
    six.append(swap(held[4][cut:], "replica", 2))
    near = [held[0], held[2], held[4], *six]
    held_all = near + [swap(h, "replica", 1) for h in near]
    by_share = inputs.reshape(row_tiles, replicas, rows_share, tokens)
    mine = pl.pallas_call(
        reorder_kernel,
        out_shape=jax.ShapeDtypeStruct(
            (replicas, held[0].shape[0] // rows_share, rows_share, tokens), jnp.bfloat16
        ),
        in_specs=smem(1) + [anywhere],
        out_specs=vmem(1)[0],
        scratch_shapes=[pltpu.SemaphoreType.DMA((replicas,))],
        name="reorder",
    )(rep ^ jnp.asarray(SHARE_ORDER, jnp.int32), by_share)
    unchanged, places = pl.pallas_call(
        functools.partial(
            unchanged_kernel, tiles_here=tiles_here, list_row=matrix.shape[0]
        ),
        out_shape=[
            jax.ShapeDtypeStruct((tokens, width), jnp.float32),
            jax.ShapeDtypeStruct((replicas, LANES), jnp.int32),
        ],
        in_specs=vmem(1 + len(held_all)),
        out_specs=vmem(2),
        name="unchanged",
    )(mine.reshape(-1, tokens), *held_all)

    low = low_rows().astype(np.float32)
    at_once = 5
    sum_rows = -(-row_tiles * KEEP // LANES) * LANES
    along = np.kron(np.eye(at_once, dtype=np.float32), low)
    along_high, along_low = split_bf16(along)
    lows = pl.pallas_call(
        functools.partial(lows_kernel, span=at_once * TILE),
        out_shape=jax.ShapeDtypeStruct((tokens, sum_rows), jnp.bfloat16),
        in_specs=vmem(3),
        out_specs=vmem(1)[0],
        scratch_shapes=[pltpu.VMEM((sum_rows, tokens), jnp.float32)],
        name="lows",
    )(inputs, along_high, along_low)

    two = jnp.concatenate([quads[None], swap(quads[None], "tok", 2)], axis=0)
    four = jnp.concatenate([two, swap(two, "tok", 1)], axis=0)
    brought = {0: four}
    brought[2] = swap(four, "replica", 2)
    brought[4] = swap(four, "replica", 4)
    brought[6] = swap(brought[2], "replica", 4)
    for o in (0, 2, 4, 6):
        brought[o ^ 1] = swap(brought[o], "replica", 1)
    early = len(SHARE_ORDER) - 2
    begun = pl.pallas_call(
        functools.partial(begin_kernel, at=range(early)),
        out_shape=jax.ShapeDtypeStruct((col_tiles // 4 * sum_rows, LANES), jnp.float32),
        in_specs=smem(1) + vmem(early),
        out_specs=vmem(1)[0],
        compiler_params=room(12),
        name="begin",
    )(places, *[brought[o] for o in SHARE_ORDER[:early]])
    across = np.kron(np.eye(col_tiles, dtype=np.float32), low).astype(jnp.bfloat16)
    values = pl.pallas_call(
        functools.partial(last_kernel, at=range(early, len(SHARE_ORDER))),
        out_shape=jax.ShapeDtypeStruct((tokens, width), jnp.bfloat16),
        in_specs=smem(1) + vmem(4 + len(SHARE_ORDER) - early),
        out_specs=vmem(1)[0],
        scratch_shapes=[pltpu.VMEM(begun.shape, jnp.float32)],
        compiler_params=room(12),
        name="last",
    )(places, lows, unchanged, across, begun, *[brought[o] for o in SHARE_ORDER[early:]])
    return (values, new_momentum)


def solution(mesh):
    return jax.shard_map(
        local,
        mesh=mesh,
        in_specs=(
            P(("replica", "tok"), None),
            P(("replica", "tok"), None),
            P(("replica", "tok"), None),
            P("tok", None),
            P("replica", "tok", None),
            P("replica", "tok", None),
            P("replica", "tok"),
        ),
        out_specs=(P(("replica", "tok"), None), P("replica", "tok", None)),
        check_vma=False,
    )
```

```python
import functools
import math

import jax
import jax.numpy as jnp
import numpy as np
from jax import lax
from jax.experimental import pallas as pl
from jax.experimental.pallas import tpu as pltpu
from jax.sharding import PartitionSpec as P


TILE = 64
KEEP = 32
LANES = 128


momentum_decay = 0.9
step_size = 0.01

HIGHEST = lax.Precision.HIGHEST

TOK_ORDER = (0, 2, 1, 3)
SHARE_ORDER = (0, 2, 4, 1, 3, 5, 6, 7)
HELD_ORDER = (0, 2, 4, 6, 1, 3, 5, 7)


def cosine_rows(count):
    frequency = jnp.arange(count, dtype=jnp.float32)[:, None]
    position = jnp.arange(TILE, dtype=jnp.float32)[None, :]
    cosines = jnp.cos(math.pi * (2.0 * position + 1.0) * frequency / (2.0 * TILE))
    factor = jnp.where(frequency == 0, math.sqrt(1.0 / TILE), math.sqrt(2.0 / TILE))
    return cosines * factor


def rebuild(summed, weight_part, keep_rows):
    quads = summed.reshape(summed.shape[0], KEEP, KEEP)
    update = jnp.einsum("ua,tuv,vb->tab", keep_rows, quads, keep_rows, precision=HIGHEST)
    shifted = weight_part.astype(jnp.float32) - step_size * update.reshape(
        summed.shape[0], TILE * TILE
    )
    return shifted.astype(jnp.bfloat16)


def forward(inputs, new_tiles):
    row_tiles = inputs.shape[1] // TILE
    col_tiles = new_tiles.shape[0] // row_tiles
    blocks = inputs.reshape(inputs.shape[0], row_tiles, TILE)
    matrix = new_tiles.reshape(row_tiles, col_tiles, TILE, TILE)
    output = jnp.einsum("tra,rcab->tcb", blocks, matrix, preferred_element_type=jnp.float32)
    return output.reshape(inputs.shape[0], col_tiles * TILE).astype(jnp.bfloat16)


def general(activations, cotangent, next_inputs, weight_tiles, momentum, chosen, counts):
    shards = lax.axis_size("tok")
    tiles_here = weight_tiles.shape[0]
    row_tiles = activations.shape[1] // TILE
    col_tiles = cotangent.shape[1] // TILE
    grad_scale = 1.0 / math.sqrt(activations.shape[0] * shards)
    keep_rows = cosine_rows(KEEP)
    product = (
        lax.dot_general(
            activations, cotangent, (((0,), (0,)), ((), ())), preferred_element_type=jnp.float32
        )
        * grad_scale
    )
    tiled = product.reshape(row_tiles, TILE, col_tiles, TILE).transpose(0, 2, 1, 3)
    tiled = tiled.reshape(row_tiles * col_tiles, TILE * TILE)
    gradient = lax.psum_scatter(
        tiled.astype(jnp.bfloat16), "tok", scatter_dimension=0, tiled=True
    ).astype(jnp.float32)
    updated = momentum_decay * momentum[0] + gradient
    chosen_here = chosen[0, 0]
    in_list = jnp.arange(chosen_here.shape[0], dtype=jnp.int32) < counts[0, 0]
    picked = jnp.take(updated, chosen_here, axis=0).reshape(-1, TILE, TILE)
    quadrant = jnp.einsum("ua,nab,vb->nuv", keep_rows, picked, keep_rows, precision=HIGHEST)
    quadrant = jnp.where(in_list[:, None, None], quadrant, 0.0).astype(jnp.bfloat16)
    rebuilt = jnp.einsum(
        "ua,nuv,vb->nab", keep_rows, quadrant.astype(jnp.float32), keep_rows, precision=HIGHEST
    )
    new_momentum = updated.at[chosen_here].add(-rebuilt.reshape(-1, TILE * TILE))
    listed = jnp.where(in_list, chosen_here, -1)
    flat_quads = quadrant.reshape(-1, KEEP * KEEP)
    tile_numbers = jnp.arange(tiles_here, dtype=jnp.int32)
    all_quads, all_listed = (
        lax.all_gather(flat_quads, "replica", axis=0, tiled=True),
        lax.all_gather(listed, "replica", axis=0, tiled=True),
    )
    one_hot = (all_listed[:, None] == tile_numbers[None, :]).astype(jnp.bfloat16)
    summed = lax.dot_general(
        one_hot, all_quads, (((0,), (0,)), ((), ())), preferred_element_type=jnp.float32
    )
    new_part = rebuild(summed, weight_tiles, keep_rows)
    new_full = lax.all_gather(new_part, "tok", axis=0, tiled=True)
    values = forward(next_inputs, new_full)
    return (values, new_momentum[None])


def low_rows():
    u = np.arange(KEEP)[:, None].astype(np.float64)
    i = np.arange(TILE)[None, :].astype(np.float64)
    factor = np.where(u == 0, math.sqrt(1.0 / TILE), math.sqrt(2.0 / TILE))
    return np.cos(math.pi * (2 * i + 1) * u / (2 * TILE)) * factor


def tables():
    low = low_rows()
    split = np.concatenate([low[:, 0::2], low[:, 1::2]], axis=0)
    into = np.zeros((4 * LANES, LANES))
    back = np.zeros((LANES, 4 * LANES))
    for g in range(4):
        into[g * LANES : g * LANES + TILE, g * KEEP : (g + 1) * KEEP] = low.T
        for half in range(2):
            at = g * LANES + half * TILE
            back[g * KEEP : (g + 1) * KEEP, at : at + TILE] = low
    split_back = np.concatenate([low[:, 0::2].T, low[:, 1::2].T], axis=0)
    return [t.astype(np.float32) for t in (split, into, split_back, back)]


def lane_index(shape):
    return lax.broadcasted_iota(jnp.int32, shape, len(shape) - 1)


def tile_products(act_ref, cot_ref, sent_ref, cot_row, grid_ref, tiled_ref, scale, spans):
    tokens = act_ref.shape[1]
    width = cot_ref.shape[1]
    first_half = lane_index((KEEP, LANES)) < TILE
    step = 2 * TILE
    theirs = [
        sent_ref[0][cot_row + n * tokens : cot_row + (n + 1) * tokens, :]
        for n in range(width // tokens)
    ]
    for block in range(spans // 2):
        rows = slice(block * step, (block + 1) * step)
        mine = jnp.dot(act_ref[rows, :], cot_ref[...], preferred_element_type=jnp.float32)
        other = sent_ref[1][rows, :]
        for n, piece in enumerate(theirs):
            lanes = slice(n * tokens, (n + 1) * tokens)
            theirs_here = jnp.dot(other, piece, preferred_element_type=jnp.float32)
            both = (mine[:, lanes] + theirs_here) * scale
            for m in range(tokens // LANES):
                grid_ref[n * (tokens // LANES) + m] = both[:, m * LANES : (m + 1) * LANES]
        for half in range(2):
            for m in range(width // LANES):
                even = grid_ref[m, pl.ds(half * TILE, KEEP, stride=2), :]
                odd = grid_ref[m, pl.ds(half * TILE + 1, KEEP, stride=2), :]
                tile = (2 * block + half) * (width // TILE) + 2 * m
                tiled_ref[tile * KEEP : (tile + 1) * KEEP, :] = jnp.where(
                    first_half, even, pltpu.roll(odd, TILE, 1)
                )
                tiled_ref[(tile + 1) * KEEP : (tile + 2) * KEEP, :] = jnp.where(
                    first_half, pltpu.roll(even, TILE, 1), odd
                )


def to_low(picked, split_ref, into_ref):
    wide = jnp.concatenate(picked, axis=1)
    mixed = jnp.dot(split_ref[...], wide, preferred_element_type=jnp.float32)
    out = []
    for h in range(len(picked) // 4):
        pieces = []
        for g in range(4):
            lanes = slice((4 * h + g) * LANES, (4 * h + g + 1) * LANES)
            pieces.append(mixed[:KEEP, lanes] + pltpu.roll(mixed[KEEP:, lanes], TILE, 1))
        row = jnp.concatenate(pieces, axis=1)
        out.append(jnp.dot(row, into_ref[...], preferred_element_type=jnp.float32))
    return out


def far_kernel(
    chosen_ref, act_ref, cot_ref, sent_ref, split_ref, into_ref,
    low_ref, *rest, scale, spans, tiles_here,
):
    sum_refs, (grid_ref, tiled_ref) = rest[:-2], rest[-2:]
    skip = first_skip(lax.axis_index("tok") ^ 2, tiles_here, cot_ref.shape[1] // TILE)
    tile_products(
        act_ref, cot_ref, (sent_ref, sent_ref), spans * TILE, grid_ref, tiled_ref, scale, spans
    )
    slots = chosen_ref.shape[0]
    picked = [
        tiled_ref[pl.ds(pl.multiple_of((skip + chosen_ref[s]) * KEEP, KEEP), KEEP), :]
        for s in range(slots)
    ]
    for h, part in enumerate(to_low(picked, split_ref, into_ref)):
        low_ref[h * KEEP : (h + 1) * KEEP, :] = part
    first = 0
    for sum_ref in sum_refs:
        rows = sum_ref.shape[0]
        for c in range(0, rows, 2 * KEEP):
            n = min(2 * KEEP, rows - c)
            sum_ref[c : c + n, :] = tiled_ref[
                pl.ds(pl.multiple_of(skip * KEEP + first + c, KEEP), n), :
            ].astype(jnp.bfloat16)
        first += rows


def factor_lows_kernel(
    chosen_ref, other_ref, mom_ref, act_ref, cot_ref, along_high_ref, along_low_ref,
    back_high_ref, back_low_ref, split_ref, into_ref,
    mine_ref, theirs_ref, high_ref, low_ref, all_ref, held_ref, sems, *, scale, tiles_here,
):
    slots = chosen_ref.shape[0]
    copies = [
        pltpu.make_async_copy(
            mom_ref.at[pl.ds(pl.multiple_of(chosen_ref[s] * KEEP, KEEP), KEEP)],
            held_ref.at[s], sems.at[s],
        )
        for s in range(slots)
    ]
    for copy in copies:
        copy.start()
    span, half = along_high_ref.shape[1], along_high_ref.shape[0]
    for c in range(act_ref.shape[0] // span):
        piece = act_ref[c * span : (c + 1) * span, :]
        rows = slice(c * half, (c + 1) * half)
        whole = jnp.dot(
            along_high_ref[...], piece, preferred_element_type=jnp.float32
        ) + jnp.dot(along_low_ref[...], piece, preferred_element_type=jnp.float32)
        high_ref[rows, :] = whole.astype(jnp.bfloat16)
        low_ref[rows, :] = (whole - whole.astype(jnp.bfloat16).astype(jnp.float32)).astype(
            jnp.bfloat16
        )
    cot_low = jnp.dot(
        cot_ref[...], back_high_ref[...], preferred_element_type=jnp.float32
    ) + jnp.dot(cot_ref[...], back_low_ref[...], preferred_element_type=jnp.float32)
    cot_low = cot_low * scale
    cot_high = cot_low.astype(jnp.bfloat16)
    cot_rest = (cot_low - cot_high.astype(jnp.float32)).astype(jnp.bfloat16)
    for c in range(0, high_ref.shape[0], half):
        rows = slice(c, c + half)
        product = (
            jnp.dot(high_ref[rows, :], cot_high, preferred_element_type=jnp.float32)
            + jnp.dot(low_ref[rows, :], cot_high, preferred_element_type=jnp.float32)
            + jnp.dot(high_ref[rows, :], cot_rest, preferred_element_type=jnp.float32)
        )
        for n in range(all_ref.shape[0]):
            all_ref[n, rows, :] = product[:, n * LANES : (n + 1) * LANES]
    group = lane_index((KEEP, LANES)) // KEEP
    me = lax.axis_index("tok")
    for copy in copies:
        copy.wait()
    own_lows = to_low([momentum_decay * held_ref[s] for s in range(slots)], split_ref, into_ref)
    for list_ref, shard, out_ref in ((chosen_ref, me, mine_ref), (other_ref, me ^ 1, theirs_ref)):
        for h in range(slots // 4):
            total = jnp.zeros((KEEP, LANES), jnp.float32)
            for g in range(4):
                tile = shard * tiles_here + list_ref[4 * h + g]
                i, j = lax.shift_right_logical(tile, 3), tile & 7
                block = all_ref[
                    lax.shift_right_logical(j, 2), pl.ds(pl.multiple_of(i * KEEP, KEEP), KEEP), :
                ]
                moved = pltpu.roll(block, (g - (j & 3)) * KEEP & (LANES - 1), 1)
                total = jnp.where(group == g, moved, total)
            if out_ref is mine_ref:
                total = total + own_lows[h]
            out_ref[h * KEEP : (h + 1) * KEEP, :] = total


def own_kernel(
    chosen_ref, mom_ref, act_ref, cot_ref, sent_ref, near_ref, quad_ref, split_back_ref,
    back_ref, *rest, scale, spans, tiles_here,
):
    sums, (out_ref, grid_ref, tiled_ref, held_ref, sem) = rest[:-5], rest[-5:]
    copy = pltpu.make_async_copy(mom_ref, held_ref, sem.at[0])
    copy.start()
    skip = first_skip(lax.axis_index("tok"), tiles_here, cot_ref.shape[1] // TILE)
    tile_products(
        act_ref, cot_ref, (sent_ref, near_ref), spans * TILE, grid_ref, tiled_ref, scale, spans
    )
    first_half = lax.rem(lane_index((KEEP, 4 * LANES)), LANES) < TILE
    for h in range(quad_ref.shape[0] // KEEP):
        quad = quad_ref[h * KEEP : (h + 1) * KEEP, :].astype(jnp.float32)
        wide = jnp.dot(quad, back_ref[...], preferred_element_type=jnp.float32)
        both = jnp.dot(split_back_ref[...], wide, preferred_element_type=jnp.float32)
        rebuilt = jnp.where(first_half, both[:KEEP, :], both[KEEP:, :])
        for g in range(4):
            at = pl.multiple_of((skip + chosen_ref[4 * h + g]) * KEEP, KEEP)
            place = pl.ds(at, KEEP)
            tiled_ref[place, :] = tiled_ref[place, :] - rebuilt[:, g * LANES : (g + 1) * LANES]
    copy.wait()
    first = 0
    for ref in sums:
        for c in range(0, ref.shape[0], 2 * KEEP):
            n = min(2 * KEEP, ref.shape[0] - c)
            rows = slice(first + c, first + c + n)
            at = pl.ds(pl.multiple_of(skip * KEEP + first + c, KEEP), n)
            out_ref[rows, :] = (
                momentum_decay * held_ref[rows, :]
                + tiled_ref[at, :]
                + ref[c : c + n, :].astype(jnp.float32)
            )
        first += ref.shape[0]


def first_row(shard, tiles_here, col_tiles):
    return pl.multiple_of((shard * tiles_here) // col_tiles * TILE, TILE)


def first_skip(shard, tiles_here, col_tiles):
    return lax.rem(shard * tiles_here, col_tiles)


def run_copies(pairs, sems):
    copies = [pltpu.make_async_copy(a, b, sems.at[n]) for n, (a, b) in enumerate(pairs)]
    for copy in copies:
        copy.start()
    for copy in copies:
        copy.wait()


def prepare_kernel(act_ref, cot_ref, far_ref, near_ref, sems, *, tiles_here):
    rows, tokens = near_ref.shape
    me = lax.axis_index("tok")
    pick = lambda n: act_ref.at[pl.ds(first_row(me ^ n, tiles_here, cot_ref.shape[1] // TILE), rows)]
    pairs = [(pick(3), far_ref.at[pl.ds(0, rows)]), (pick(1), near_ref)]
    for n in range(cot_ref.shape[1] // tokens):
        lanes, at = pl.ds(n * tokens, tokens), pl.ds(rows + n * tokens, tokens)
        pairs.append((cot_ref.at[:, lanes], far_ref.at[at]))
    run_copies(pairs, sems)


def mine_kernel(act_ref, far_ref, near_ref, sems, *, tiles_here, col_tiles):
    me, rows = lax.axis_index("tok"), near_ref.shape[0]
    pick = lambda n: act_ref.at[pl.ds(first_row(me ^ n, tiles_here, col_tiles), rows)]
    run_copies([(pick(2), far_ref), (pick(0), near_ref)], sems)


def unchanged_kernel(inputs_ref, *refs, tiles_here, list_row):
    count = len(HELD_ORDER)
    held, (out_ref, place_ref), rest = refs[:count], refs[count : count + 2], refs[count + 2 :]
    mine_ref, held_refs, sems = rest[0], rest[1:-1], rest[-1]
    rep, me = lax.axis_index("replica"), lax.axis_index("tok")
    used = inputs_ref.shape[0]
    mine_copies = [
        pltpu.make_async_copy(
            inputs_ref.at[:, rep ^ o], mine_ref.at[n, pl.ds(0, used)], sems.at[count + n]
        )
        for n, o in enumerate(SHARE_ORDER)
    ]
    copies = [
        pltpu.make_async_copy(a, b, sems.at[n]) for n, (a, b) in enumerate(zip(held, held_refs))
    ]
    for n, o in enumerate(SHARE_ORDER):
        mine_copies[n].start()
        for copy, k in zip(copies, HELD_ORDER):
            if k == o:
                copy.start()
    for n in range(used, mine_ref.shape[1]):
        mine_ref[:, n] = jnp.zeros_like(mine_ref[:, n])
    size = held_refs[0].shape[0]
    lane = lane_index((1, LANES))
    total = None
    for n, o in enumerate(SHARE_ORDER):
        mine_copies[n].wait()
        x = mine_ref[n].reshape(size, mine_ref.shape[3])
        first = 0
        for copy, k, piece in zip(copies, HELD_ORDER, held_refs):
            if k != o:
                continue
            copy.wait()
            term = lax.dot_general(
                x[first : first + piece.shape[0], :], piece[...], (((0,), (0,)), ((), ())),
                preferred_element_type=jnp.float32,
            )
            first += piece.shape[0]
            total = term if total is None else total + term
            last = piece
        at = list_row - (size - last.shape[0])
        lists = last[at : at + 8, :LANES].astype(jnp.float32).astype(jnp.int32)
        row = jnp.zeros((1, LANES), jnp.int32)
        for d, offset in enumerate(TOK_ORDER):
            tile = lists[d : d + 1, :] + (me ^ offset) * tiles_here
            i, j = lax.shift_right_logical(tile, 3), tile & 7
            packed = (lax.shift_right_logical(j, 2) * place_rows(used) + i * KEEP) * LANES
            packed = packed + (j & 3) * KEEP
            packed = pltpu.roll(packed, 8 * d, 1)
            row = jnp.where((lane >= 8 * d) & (lane < 8 * (d + 1)), packed, row)
        place_ref[n : n + 1, :] = row
    out_ref[...] = total


def place_rows(row_tiles):
    return -(-(row_tiles * KEEP) // LANES) * LANES


def lows_kernel(inputs_ref, high_ref, low_ref, out_ref, lows_ref, *, span):
    rows = inputs_ref.shape[0]
    half = span // 2
    lows_ref[...] = jnp.zeros_like(lows_ref)
    for c in range(rows // span):
        piece = inputs_ref[c * span : (c + 1) * span, :]
        lows_ref[c * half : (c + 1) * half, :] = jnp.dot(
            high_ref[...], piece, preferred_element_type=jnp.float32
        ) + jnp.dot(low_ref[...], piece, preferred_element_type=jnp.float32)
    out_ref[...] = lows_ref[...].T.astype(jnp.bfloat16)


def add_quads(place_ref, n, quads_ref, sum_ref):
    first_lane = lane_index((KEEP, LANES)) // KEEP * KEEP
    slots = quads_ref.shape[1] // KEEP * 4

    def add_list(d, carry):
        puts = []
        for s in range(slots):
            h, g = s // 4, s % 4
            quad = quads_ref[d, h * KEEP : (h + 1) * KEEP, :]
            packed = place_ref[n, d * slots + s]
            to = packed & (LANES - 1)
            moved = pltpu.roll(quad.astype(jnp.float32), (to - g * KEEP) & (LANES - 1), 1)
            row = pl.multiple_of(lax.shift_right_logical(packed, 7), KEEP)
            place = sum_ref.at[pl.ds(row, KEEP)]
            puts.append((place, place[...] + moved, first_lane == to))
        for place, value, mask in puts:
            pltpu.store(place, value, mask=mask)
        return carry

    lax.fori_loop(0, quads_ref.shape[0], add_list, 0)


def last_kernel(place_ref, lows_ref, base_ref, across_ref, *refs):
    quads, (out_ref, sum_ref) = refs[:-2], refs[-2:]
    sum_ref[...] = jnp.zeros_like(sum_ref)
    for n, ref in enumerate(quads):
        add_quads(place_ref, n, ref, sum_ref)
    rows = lows_ref.shape[1]
    whole = jnp.concatenate(
        [
            sum_ref[n * rows : (n + 1) * rows, :].astype(jnp.bfloat16)
            for n in range(sum_ref.shape[0] // rows)
        ],
        axis=1,
    )
    mixed = jnp.dot(lows_ref[...], whole, preferred_element_type=jnp.float32)
    update = jnp.dot(
        mixed.astype(jnp.bfloat16), across_ref[...], preferred_element_type=jnp.float32
    )
    out_ref[...] = (base_ref[...] - step_size * update).astype(jnp.bfloat16)


def split_bf16(table):
    top = table.astype(jnp.bfloat16)
    return top, (table - top.astype(np.float32)).astype(jnp.bfloat16)


def room(mib):
    return pltpu.CompilerParams(vmem_limit_bytes=mib * 1024 * 1024)


def vmem(count):
    return [pl.BlockSpec(memory_space=pltpu.VMEM)] * count


def smem(count):
    return [pl.BlockSpec(memory_space=pltpu.SMEM)] * count


def swap(array, axis, bit):
    size = lax.axis_size(axis)
    return lax.ppermute(array, axis, [(i, i ^ bit) for i in range(size)])


def fits(shards, replicas, activations, cotangent, weight_tiles, slots):
    tokens, depth = activations.shape
    width = cotangent.shape[1]
    tiles_here = weight_tiles.shape[0]
    span = span_of(tiles_here, width // TILE)
    return (
        shards == 4
        and replicas == 8
        and tokens % LANES == 0
        and width % tokens == 0
        and width // TILE == 8
        and slots == 8
        and depth % (5 * TILE) == 0
        and tiles_here % 10 == 0
        and tiles_here <= 256
        and slots <= 128
        and span % 2 == 0
        and all((n * tiles_here) // 8 + span <= depth // TILE for n in range(shards))
        and all((n * tiles_here) % 8 + tiles_here <= span * 8 for n in range(shards))
    )


def span_of(tiles_here, col_tiles):
    return 2 * (-(-tiles_here // col_tiles) // 2)


def local(activations, cotangent, next_inputs, weight_tiles, momentum, chosen, counts):
    shards = lax.axis_size("tok")
    replicas = lax.axis_size("replica")
    slots = chosen.shape[-1]
    if not fits(shards, replicas, activations, cotangent, weight_tiles, slots):
        return general(
            activations, cotangent, next_inputs, weight_tiles, momentum, chosen, counts
        )
    return four_shards(
        activations, cotangent, next_inputs, weight_tiles, momentum, chosen, counts
    )


def four_shards(activations, cotangent, next_inputs, weight_tiles, momentum, chosen, counts):
    shards = lax.axis_size("tok")
    replicas = lax.axis_size("replica")
    slots = chosen.shape[-1]
    tokens, depth = activations.shape
    width = cotangent.shape[1]
    tiles_here = weight_tiles.shape[0]
    row_tiles = depth // TILE
    col_tiles = width // TILE
    spans = span_of(tiles_here, col_tiles)
    span_rows = spans * TILE
    scale = 1.0 / math.sqrt(tokens * shards)
    me = lax.axis_index("tok")
    rep = lax.axis_index("replica")
    act = activations.T
    inputs = next_inputs.T
    split, into, split_back, back = tables()

    def place_of(offset):
        return (offset & 1) * 2 + lax.shift_right_logical(offset, 1)

    anywhere = pl.BlockSpec(memory_space=pltpu.HBM)
    share = TILE * TILE // replicas
    listed = chosen[0, 0].astype(jnp.bfloat16)
    pad_rows = -(tiles_here + 1) % 8 + 1
    piece = jnp.concatenate(
        [
            lax.dynamic_slice(weight_tiles, (0, rep * share), (tiles_here, share)),
            jnp.zeros((pad_rows, share), jnp.bfloat16).at[0, :slots].set(listed),
        ],
        axis=0,
    )[None]
    piece_far = swap(piece, "tok", 2)
    pair = jnp.concatenate([piece, piece_far], axis=0)
    pair_near = swap(pair, "tok", 1)
    sent_rows, near_rows = pl.pallas_call(
        functools.partial(prepare_kernel, tiles_here=tiles_here),
        out_shape=[
            jax.ShapeDtypeStruct((span_rows + width, tokens), jnp.bfloat16),
            jax.ShapeDtypeStruct((span_rows, tokens), jnp.bfloat16),
        ],
        in_specs=[anywhere] * 2,
        out_specs=vmem(2),
        scratch_shapes=[pltpu.SemaphoreType.DMA((2 + width // tokens,))],
        name="prepare",
    )(act, cotangent)
    sent_far = swap(sent_rows, "tok", 1)
    mine_far, mine_near = pl.pallas_call(
        functools.partial(mine_kernel, tiles_here=tiles_here, col_tiles=col_tiles),
        out_shape=[jax.ShapeDtypeStruct((span_rows, tokens), jnp.bfloat16)] * 2,
        in_specs=[anywhere],
        out_specs=vmem(2),
        scratch_shapes=[pltpu.SemaphoreType.DMA((2,))],
        name="mine",
    )(act)
    far_chosen = piece_far[0, tiles_here, :slots].astype(jnp.int32)
    near_chosen = pair_near[0, tiles_here, :slots].astype(jnp.int32)
    pieces = jnp.concatenate([pair, pair_near], axis=0)
    sent_near = swap(near_rows, "tok", 1)

    moment = momentum.reshape(tiles_here * KEEP, LANES)
    low = low_rows().astype(np.float32)
    at_once = 5
    sum_rows = place_rows(row_tiles)
    along_high, along_low = split_bf16(np.kron(np.eye(at_once, dtype=np.float32), low))
    across = np.kron(np.eye(col_tiles, dtype=np.float32), low)
    low_shape = jax.ShapeDtypeStruct((slots // 4 * KEEP, LANES), jnp.float32)
    low_mine, low_near = pl.pallas_call(
        functools.partial(factor_lows_kernel, scale=scale, tiles_here=tiles_here),
        out_shape=[low_shape] * 2,
        in_specs=smem(2) + [anywhere] + vmem(8),
        out_specs=vmem(2),
        scratch_shapes=[pltpu.VMEM((row_tiles * KEEP, tokens), jnp.bfloat16)] * 2
        + [
            pltpu.VMEM((col_tiles // 4, row_tiles * KEEP, LANES), jnp.float32),
            pltpu.VMEM((slots, KEEP, LANES), jnp.float32),
            pltpu.SemaphoreType.DMA((slots,)),
        ],
        name="factor_lows",
    )(
        chosen[0, 0], near_chosen, moment, act, cotangent, along_high, along_low,
        *split_bf16(np.ascontiguousarray(across.T)), split, into,
    )
    low_from_near = swap(low_near, "tok", 1)

    grid_scratch = [
        pltpu.VMEM((width // LANES, 2 * TILE, LANES), jnp.float32),
        pltpu.VMEM((spans * col_tiles * KEEP, LANES), jnp.float32),
    ]
    cuts = [tiles_here * 2 // 15, tiles_here // 5]
    cuts.append(tiles_here - sum(cuts))
    far_low, *far_sums = pl.pallas_call(
        functools.partial(far_kernel, scale=scale, spans=spans, tiles_here=tiles_here),
        out_shape=[low_shape]
        + [jax.ShapeDtypeStruct((n * KEEP, LANES), jnp.bfloat16) for n in cuts],
        in_specs=smem(1) + vmem(5),
        out_specs=vmem(1 + len(cuts)),
        scratch_shapes=grid_scratch,
        compiler_params=room(12),
        name="far",
    )(far_chosen, mine_far, cotangent, sent_far, split, into)
    low_from_far = swap(far_low, "tok", 2)
    sums_from = []
    for part in far_sums:
        sums_from.append(swap(part, "tok", 2))

    at = np.arange(low_shape.shape[0])[:, None] // KEEP * 4 + np.arange(LANES) // KEEP
    quads = jnp.where(
        jnp.asarray(at, jnp.int32) < counts[0, 0], low_mine + low_from_near + low_from_far, 0.0
    ).astype(jnp.bfloat16)
    new_momentum = pl.pallas_call(
        functools.partial(own_kernel, scale=scale, spans=spans, tiles_here=tiles_here),
        out_shape=jax.ShapeDtypeStruct(moment.shape, jnp.float32),
        in_specs=smem(1) + [anywhere] + vmem(7 + len(cuts)),
        out_specs=vmem(1)[0],
        scratch_shapes=grid_scratch
        + [pltpu.VMEM(moment.shape, jnp.float32), pltpu.SemaphoreType.DMA((1,))],
        name="own",
    )(
        chosen[0, 0], moment, mine_near, cotangent, sent_far, sent_near, quads, split_back,
        back, *sums_from,
    ).reshape(momentum.shape)

    whole = jnp.concatenate(
        [
            lax.dynamic_index_in_dim(pieces, place_of(me ^ n), 0, False)[:tiles_here]
            for n in range(shards)
        ],
        axis=0,
    )
    rows_share = TILE // replicas
    matrix = whole.reshape(row_tiles, col_tiles, rows_share, TILE).transpose(0, 2, 1, 3)
    matrix = matrix.reshape(row_tiles * rows_share, width)
    list_rows = jnp.zeros((8, width), jnp.bfloat16)
    list_rows = list_rows.at[:shards, :slots].set(pieces[:, tiles_here, :slots])
    held = {0: jnp.concatenate([matrix, list_rows], axis=0)}
    held[2] = swap(held[0], "replica", 2)
    held[4] = swap(held[0], "replica", 4)
    held[6] = swap(held[2], "replica", 4)
    near = [held[o] for o in (0, 2, 4, 6)]
    held_all = list(near)
    for h in near:
        held_all.append(swap(h, "replica", 1))
    by_share = inputs.reshape(row_tiles, replicas, rows_share, tokens)
    unchanged, places = pl.pallas_call(
        functools.partial(
            unchanged_kernel, tiles_here=tiles_here, list_row=matrix.shape[0]
        ),
        out_shape=[
            jax.ShapeDtypeStruct((tokens, width), jnp.float32),
            jax.ShapeDtypeStruct((replicas, LANES), jnp.int32),
        ],
        in_specs=[anywhere] * (1 + len(held_all)),
        out_specs=vmem(2),
        scratch_shapes=[
            pltpu.VMEM((replicas, held[0].shape[0] // rows_share, rows_share, tokens), jnp.bfloat16)
        ]
        + [pltpu.VMEM(h.shape, jnp.bfloat16) for h in held_all]
        + [pltpu.SemaphoreType.DMA((replicas + len(held_all),))],
        name="unchanged",
    )(by_share, *held_all)

    lows = pl.pallas_call(
        functools.partial(lows_kernel, span=at_once * TILE),
        out_shape=jax.ShapeDtypeStruct((tokens, sum_rows), jnp.bfloat16),
        in_specs=vmem(3),
        out_specs=vmem(1)[0],
        scratch_shapes=[pltpu.VMEM((sum_rows, tokens), jnp.float32)],
        name="lows",
    )(inputs, along_high, along_low)

    two = jnp.concatenate([quads[None], swap(quads[None], "tok", 2)], axis=0)
    four = jnp.concatenate([two, swap(two, "tok", 1)], axis=0)
    brought = {0: four}
    brought[2] = swap(four, "replica", 2)
    brought[4] = swap(four, "replica", 4)
    brought[6] = swap(brought[2], "replica", 4)
    for o in (0, 2, 4, 6):
        brought[o ^ 1] = swap(brought[o], "replica", 1)
    values = pl.pallas_call(
        last_kernel,
        out_shape=jax.ShapeDtypeStruct((tokens, width), jnp.bfloat16),
        in_specs=smem(1) + vmem(3 + len(SHARE_ORDER)),
        out_specs=vmem(1)[0],
        scratch_shapes=[pltpu.VMEM((col_tiles // 4 * sum_rows, LANES), jnp.float32)],
        compiler_params=room(12),
        name="last",
    )(places, lows, unchanged, across.astype(jnp.bfloat16), *[brought[o] for o in SHARE_ORDER])
    return (values, new_momentum)


def solution(mesh):
    return jax.shard_map(
        local,
        mesh=mesh,
        in_specs=(
            P(("replica", "tok"), None),
            P(("replica", "tok"), None),
            P(("replica", "tok"), None),
            P("tok", None),
            P("replica", "tok", None),
            P("replica", "tok", None),
            P("replica", "tok"),
        ),
        out_specs=(P(("replica", "tok"), None), P("replica", "tok", None)),
        check_vma=False,
    )
```

```python
import functools
import math

import jax
import jax.numpy as jnp
import numpy as np
from jax import lax
from jax.experimental import pallas as pl
from jax.experimental.pallas import tpu as pltpu
from jax.sharding import PartitionSpec as P


TILE = 64
KEEP = 32
LANES = 128


momentum_decay = 0.9
step_size = 0.01

HIGHEST = lax.Precision.HIGHEST

TOK_ORDER = (0, 2, 1, 3)
SHARE_ORDER = (0, 2, 4, 1, 3, 5, 6, 7)
HELD_ORDER = (0, 2, 4, 6, 1, 3, 5, 7)


def cosine_rows(count):
    frequency = jnp.arange(count, dtype=jnp.float32)[:, None]
    position = jnp.arange(TILE, dtype=jnp.float32)[None, :]
    cosines = jnp.cos(math.pi * (2.0 * position + 1.0) * frequency / (2.0 * TILE))
    factor = jnp.where(frequency == 0, math.sqrt(1.0 / TILE), math.sqrt(2.0 / TILE))
    return cosines * factor


def rebuild(summed, weight_part, keep_rows):
    quads = summed.reshape(summed.shape[0], KEEP, KEEP)
    update = jnp.einsum("ua,tuv,vb->tab", keep_rows, quads, keep_rows, precision=HIGHEST)
    shifted = weight_part.astype(jnp.float32) - step_size * update.reshape(
        summed.shape[0], TILE * TILE
    )
    return shifted.astype(jnp.bfloat16)


def forward(inputs, new_tiles):
    row_tiles = inputs.shape[1] // TILE
    col_tiles = new_tiles.shape[0] // row_tiles
    blocks = inputs.reshape(inputs.shape[0], row_tiles, TILE)
    matrix = new_tiles.reshape(row_tiles, col_tiles, TILE, TILE)
    output = jnp.einsum("tra,rcab->tcb", blocks, matrix, preferred_element_type=jnp.float32)
    return output.reshape(inputs.shape[0], col_tiles * TILE).astype(jnp.bfloat16)


def general(activations, cotangent, next_inputs, weight_tiles, momentum, chosen, counts):
    shards = lax.axis_size("tok")
    tiles_here = weight_tiles.shape[0]
    row_tiles = activations.shape[1] // TILE
    col_tiles = cotangent.shape[1] // TILE
    grad_scale = 1.0 / math.sqrt(activations.shape[0] * shards)
    keep_rows = cosine_rows(KEEP)
    product = (
        lax.dot_general(
            activations, cotangent, (((0,), (0,)), ((), ())), preferred_element_type=jnp.float32
        )
        * grad_scale
    )
    tiled = product.reshape(row_tiles, TILE, col_tiles, TILE).transpose(0, 2, 1, 3)
    tiled = tiled.reshape(row_tiles * col_tiles, TILE * TILE)
    gradient = lax.psum_scatter(
        tiled.astype(jnp.bfloat16), "tok", scatter_dimension=0, tiled=True
    ).astype(jnp.float32)
    updated = momentum_decay * momentum[0] + gradient
    chosen_here = chosen[0, 0]
    in_list = jnp.arange(chosen_here.shape[0], dtype=jnp.int32) < counts[0, 0]
    picked = jnp.take(updated, chosen_here, axis=0).reshape(-1, TILE, TILE)
    quadrant = jnp.einsum("ua,nab,vb->nuv", keep_rows, picked, keep_rows, precision=HIGHEST)
    quadrant = jnp.where(in_list[:, None, None], quadrant, 0.0).astype(jnp.bfloat16)
    rebuilt = jnp.einsum(
        "ua,nuv,vb->nab", keep_rows, quadrant.astype(jnp.float32), keep_rows, precision=HIGHEST
    )
    new_momentum = updated.at[chosen_here].add(-rebuilt.reshape(-1, TILE * TILE))
    listed = jnp.where(in_list, chosen_here, -1)
    flat_quads = quadrant.reshape(-1, KEEP * KEEP)
    tile_numbers = jnp.arange(tiles_here, dtype=jnp.int32)
    all_quads, all_listed = (
        lax.all_gather(flat_quads, "replica", axis=0, tiled=True),
        lax.all_gather(listed, "replica", axis=0, tiled=True),
    )
    one_hot = (all_listed[:, None] == tile_numbers[None, :]).astype(jnp.bfloat16)
    summed = lax.dot_general(
        one_hot, all_quads, (((0,), (0,)), ((), ())), preferred_element_type=jnp.float32
    )
    new_part = rebuild(summed, weight_tiles, keep_rows)
    new_full = lax.all_gather(new_part, "tok", axis=0, tiled=True)
    values = forward(next_inputs, new_full)
    return (values, new_momentum[None])


def low_rows():
    u = np.arange(KEEP)[:, None].astype(np.float64)
    i = np.arange(TILE)[None, :].astype(np.float64)
    factor = np.where(u == 0, math.sqrt(1.0 / TILE), math.sqrt(2.0 / TILE))
    return np.cos(math.pi * (2 * i + 1) * u / (2 * TILE)) * factor


def tables():
    low = low_rows()
    split = np.concatenate([low[:, 0::2], low[:, 1::2]], axis=0)
    into = np.zeros((4 * LANES, LANES))
    back = np.zeros((LANES, 4 * LANES))
    for g in range(4):
        into[g * LANES : g * LANES + TILE, g * KEEP : (g + 1) * KEEP] = low.T
        for half in range(2):
            at = g * LANES + half * TILE
            back[g * KEEP : (g + 1) * KEEP, at : at + TILE] = low
    split_back = np.concatenate([low[:, 0::2].T, low[:, 1::2].T], axis=0)
    return [t.astype(np.float32) for t in (split, into, split_back, back)]


def lane_index(shape):
    return lax.broadcasted_iota(jnp.int32, shape, len(shape) - 1)


def tile_products(act_ref, cot_ref, sent_ref, cot_row, grid_ref, tiled_ref, scale, spans):
    tokens = act_ref.shape[1]
    width = cot_ref.shape[1]
    first_half = lane_index((KEEP, LANES)) < TILE
    step = 2 * TILE
    theirs = [
        sent_ref[0][cot_row + n * tokens : cot_row + (n + 1) * tokens, :]
        for n in range(width // tokens)
    ]
    for block in range(spans // 2):
        rows = slice(block * step, (block + 1) * step)
        mine = jnp.dot(act_ref[rows, :], cot_ref[...], preferred_element_type=jnp.float32)
        other = sent_ref[1][rows, :]
        for n, piece in enumerate(theirs):
            lanes = slice(n * tokens, (n + 1) * tokens)
            theirs_here = jnp.dot(other, piece, preferred_element_type=jnp.float32)
            both = (mine[:, lanes] + theirs_here) * scale
            for m in range(tokens // LANES):
                grid_ref[n * (tokens // LANES) + m] = both[:, m * LANES : (m + 1) * LANES]
        for half in range(2):
            for m in range(width // LANES):
                even = grid_ref[m, pl.ds(half * TILE, KEEP, stride=2), :]
                odd = grid_ref[m, pl.ds(half * TILE + 1, KEEP, stride=2), :]
                tile = (2 * block + half) * (width // TILE) + 2 * m
                tiled_ref[tile * KEEP : (tile + 1) * KEEP, :] = jnp.where(
                    first_half, even, pltpu.roll(odd, TILE, 1)
                )
                tiled_ref[(tile + 1) * KEEP : (tile + 2) * KEEP, :] = jnp.where(
                    first_half, pltpu.roll(even, TILE, 1), odd
                )


def to_low(picked, split_ref, into_ref):
    wide = jnp.concatenate(picked, axis=1)
    mixed = jnp.dot(split_ref[...], wide, preferred_element_type=jnp.float32)
    out = []
    for h in range(len(picked) // 4):
        pieces = []
        for g in range(4):
            lanes = slice((4 * h + g) * LANES, (4 * h + g + 1) * LANES)
            pieces.append(mixed[:KEEP, lanes] + pltpu.roll(mixed[KEEP:, lanes], TILE, 1))
        row = jnp.concatenate(pieces, axis=1)
        out.append(jnp.dot(row, into_ref[...], preferred_element_type=jnp.float32))
    return out


def far_kernel(
    chosen_ref, act_ref, cot_ref, sent_ref, split_ref, into_ref,
    low_ref, *rest, scale, spans, tiles_here,
):
    sum_refs, (grid_ref, tiled_ref) = rest[:-2], rest[-2:]
    skip = first_skip(lax.axis_index("tok") ^ 2, tiles_here, cot_ref.shape[1] // TILE)
    tile_products(
        act_ref, cot_ref, (sent_ref, sent_ref), spans * TILE, grid_ref, tiled_ref, scale, spans
    )
    slots = chosen_ref.shape[0]
    picked = [
        tiled_ref[pl.ds(pl.multiple_of((skip + chosen_ref[s]) * KEEP, KEEP), KEEP), :]
        for s in range(slots)
    ]
    for h, part in enumerate(to_low(picked, split_ref, into_ref)):
        low_ref[h * KEEP : (h + 1) * KEEP, :] = part
    first = 0
    for sum_ref in sum_refs:
        rows = sum_ref.shape[0]
        for c in range(0, rows, 2 * KEEP):
            n = min(2 * KEEP, rows - c)
            sum_ref[c : c + n, :] = tiled_ref[
                pl.ds(pl.multiple_of(skip * KEEP + first + c, KEEP), n), :
            ].astype(jnp.bfloat16)
        first += rows


def factor_lows_kernel(
    chosen_ref, other_ref, mom_ref, act_ref, cot_ref, along_high_ref, along_low_ref,
    back_high_ref, back_low_ref, split_ref, into_ref,
    mine_ref, theirs_ref, high_ref, low_ref, all_ref, held_ref, sems, *, scale, tiles_here,
):
    slots = chosen_ref.shape[0]
    copies = [
        pltpu.make_async_copy(
            mom_ref.at[pl.ds(pl.multiple_of(chosen_ref[s] * KEEP, KEEP), KEEP)],
            held_ref.at[s], sems.at[s],
        )
        for s in range(slots)
    ]
    for copy in copies:
        copy.start()
    span, half = along_high_ref.shape[1], along_high_ref.shape[0]
    for c in range(act_ref.shape[0] // span):
        piece = act_ref[c * span : (c + 1) * span, :]
        rows = slice(c * half, (c + 1) * half)
        whole = jnp.dot(
            along_high_ref[...], piece, preferred_element_type=jnp.float32
        ) + jnp.dot(along_low_ref[...], piece, preferred_element_type=jnp.float32)
        high_ref[rows, :] = whole.astype(jnp.bfloat16)
        low_ref[rows, :] = (whole - whole.astype(jnp.bfloat16).astype(jnp.float32)).astype(
            jnp.bfloat16
        )
    cot_low = jnp.dot(
        cot_ref[...], back_high_ref[...], preferred_element_type=jnp.float32
    ) + jnp.dot(cot_ref[...], back_low_ref[...], preferred_element_type=jnp.float32)
    cot_low = cot_low * scale
    cot_high = cot_low.astype(jnp.bfloat16)
    cot_rest = (cot_low - cot_high.astype(jnp.float32)).astype(jnp.bfloat16)
    for c in range(0, high_ref.shape[0], half):
        rows = slice(c, c + half)
        product = (
            jnp.dot(high_ref[rows, :], cot_high, preferred_element_type=jnp.float32)
            + jnp.dot(low_ref[rows, :], cot_high, preferred_element_type=jnp.float32)
            + jnp.dot(high_ref[rows, :], cot_rest, preferred_element_type=jnp.float32)
        )
        for n in range(all_ref.shape[0]):
            all_ref[n, rows, :] = product[:, n * LANES : (n + 1) * LANES]
    group = lane_index((KEEP, LANES)) // KEEP
    me = lax.axis_index("tok")
    for copy in copies:
        copy.wait()
    own_lows = to_low([momentum_decay * held_ref[s] for s in range(slots)], split_ref, into_ref)
    for list_ref, shard, out_ref in ((chosen_ref, me, mine_ref), (other_ref, me ^ 1, theirs_ref)):
        for h in range(slots // 4):
            total = jnp.zeros((KEEP, LANES), jnp.float32)
            for g in range(4):
                tile = shard * tiles_here + list_ref[4 * h + g]
                i, j = lax.shift_right_logical(tile, 3), tile & 7
                block = all_ref[
                    lax.shift_right_logical(j, 2), pl.ds(pl.multiple_of(i * KEEP, KEEP), KEEP), :
                ]
                moved = pltpu.roll(block, (g - (j & 3)) * KEEP & (LANES - 1), 1)
                total = jnp.where(group == g, moved, total)
            if out_ref is mine_ref:
                total = total + own_lows[h]
            out_ref[h * KEEP : (h + 1) * KEEP, :] = total


def own_kernel(
    chosen_ref, mom_ref, act_ref, cot_ref, sent_ref, near_ref, quad_ref, split_back_ref,
    back_ref, *rest, scale, spans, tiles_here,
):
    sums, (out_ref, grid_ref, tiled_ref, held_ref, sem) = rest[:-5], rest[-5:]
    copy = pltpu.make_async_copy(mom_ref, held_ref, sem.at[0])
    copy.start()
    skip = first_skip(lax.axis_index("tok"), tiles_here, cot_ref.shape[1] // TILE)
    tile_products(
        act_ref, cot_ref, (sent_ref, near_ref), spans * TILE, grid_ref, tiled_ref, scale, spans
    )
    first_half = lax.rem(lane_index((KEEP, 4 * LANES)), LANES) < TILE
    for h in range(quad_ref.shape[0] // KEEP):
        quad = quad_ref[h * KEEP : (h + 1) * KEEP, :].astype(jnp.float32)
        wide = jnp.dot(quad, back_ref[...], preferred_element_type=jnp.float32)
        both = jnp.dot(split_back_ref[...], wide, preferred_element_type=jnp.float32)
        rebuilt = jnp.where(first_half, both[:KEEP, :], both[KEEP:, :])
        for g in range(4):
            at = pl.multiple_of((skip + chosen_ref[4 * h + g]) * KEEP, KEEP)
            place = pl.ds(at, KEEP)
            tiled_ref[place, :] = tiled_ref[place, :] - rebuilt[:, g * LANES : (g + 1) * LANES]
    copy.wait()
    first = 0
    for ref in sums + (None,):
        size = out_ref.shape[0] - first if ref is None else ref.shape[0]
        for c in range(0, size, 2 * KEEP):
            n = min(2 * KEEP, size - c)
            rows = slice(first + c, first + c + n)
            at = pl.ds(pl.multiple_of(skip * KEEP + first + c, KEEP), n)
            value = momentum_decay * held_ref[rows, :] + tiled_ref[at, :]
            if ref is not None:
                value = value + ref[c : c + n, :].astype(jnp.float32)
            out_ref[rows, :] = value
        first += size


def finish_kernel(base_ref, sum_ref, out_ref):
    first = base_ref.shape[0] - sum_ref.shape[0]
    for c in range(0, base_ref.shape[0], KEEP):
        value = base_ref[c : c + KEEP, :]
        if c >= first:
            value = value + sum_ref[c - first : c - first + KEEP, :].astype(jnp.float32)
        out_ref[c : c + KEEP, :] = value


def first_row(shard, tiles_here, col_tiles):
    return pl.multiple_of((shard * tiles_here) // col_tiles * TILE, TILE)


def first_skip(shard, tiles_here, col_tiles):
    return lax.rem(shard * tiles_here, col_tiles)


def run_copies(pairs, sems):
    copies = [pltpu.make_async_copy(a, b, sems.at[n]) for n, (a, b) in enumerate(pairs)]
    for copy in copies:
        copy.start()
    for copy in copies:
        copy.wait()


def prepare_kernel(act_ref, cot_ref, far_ref, near_ref, sems, *, tiles_here):
    rows, tokens = near_ref.shape
    me = lax.axis_index("tok")
    pick = lambda n: act_ref.at[pl.ds(first_row(me ^ n, tiles_here, cot_ref.shape[1] // TILE), rows)]
    pairs = [(pick(3), far_ref.at[pl.ds(0, rows)]), (pick(1), near_ref)]
    for n in range(cot_ref.shape[1] // tokens):
        lanes, at = pl.ds(n * tokens, tokens), pl.ds(rows + n * tokens, tokens)
        pairs.append((cot_ref.at[:, lanes], far_ref.at[at]))
    run_copies(pairs, sems)


def mine_kernel(act_ref, far_ref, near_ref, sems, *, tiles_here, col_tiles):
    me, rows = lax.axis_index("tok"), near_ref.shape[0]
    pick = lambda n: act_ref.at[pl.ds(first_row(me ^ n, tiles_here, col_tiles), rows)]
    run_copies([(pick(2), far_ref), (pick(0), near_ref)], sems)


def unchanged_kernel(inputs_ref, *refs, tiles_here, list_row):
    count = len(HELD_ORDER)
    held, (out_ref, place_ref), rest = refs[:count], refs[count : count + 2], refs[count + 2 :]
    (mine_ref, sems), held_refs = rest, held
    rep, me = lax.axis_index("replica"), lax.axis_index("tok")
    used = inputs_ref.shape[0]
    mine_copies = [
        pltpu.make_async_copy(
            inputs_ref.at[:, rep ^ o], mine_ref.at[n, pl.ds(0, used)], sems.at[n]
        )
        for n, o in enumerate(SHARE_ORDER)
    ]
    for copy in mine_copies:
        copy.start()
    for n in range(used, mine_ref.shape[1]):
        mine_ref[:, n] = jnp.zeros_like(mine_ref[:, n])
    size = held_refs[0].shape[0]
    lane = lane_index((1, LANES))
    total = None
    for n, o in enumerate(SHARE_ORDER):
        mine_copies[n].wait()
        x = mine_ref[n].reshape(size, mine_ref.shape[3])
        first = 0
        for k, piece in zip(HELD_ORDER, held_refs):
            if k != o:
                continue
            term = lax.dot_general(
                x[first : first + piece.shape[0], :], piece[...], (((0,), (0,)), ((), ())),
                preferred_element_type=jnp.float32,
            )
            first += piece.shape[0]
            total = term if total is None else total + term
            last = piece
        at = list_row - (size - last.shape[0])
        lists = last[at : at + 8, :LANES].astype(jnp.float32).astype(jnp.int32)
        row = jnp.zeros((1, LANES), jnp.int32)
        for d, offset in enumerate(TOK_ORDER):
            tile = lists[d : d + 1, :] + (me ^ offset) * tiles_here
            i, j = lax.shift_right_logical(tile, 3), tile & 7
            packed = (lax.shift_right_logical(j, 2) * place_rows(used) + i * KEEP) * LANES
            packed = packed + (j & 3) * KEEP
            packed = pltpu.roll(packed, 8 * d, 1)
            row = jnp.where((lane >= 8 * d) & (lane < 8 * (d + 1)), packed, row)
        place_ref[n : n + 1, :] = row
    out_ref[...] = total


def place_rows(row_tiles):
    return -(-(row_tiles * KEEP) // LANES) * LANES


def lows_kernel(inputs_ref, high_ref, low_ref, out_ref, lows_ref, *, span):
    rows = inputs_ref.shape[0]
    half = span // 2
    lows_ref[...] = jnp.zeros_like(lows_ref)
    for c in range(rows // span):
        piece = inputs_ref[c * span : (c + 1) * span, :]
        lows_ref[c * half : (c + 1) * half, :] = jnp.dot(
            high_ref[...], piece, preferred_element_type=jnp.float32
        ) + jnp.dot(low_ref[...], piece, preferred_element_type=jnp.float32)
    out_ref[...] = lows_ref[...].T.astype(jnp.bfloat16)


def add_quads(place_ref, n, quads_ref, sum_ref):
    first_lane = lane_index((KEEP, LANES)) // KEEP * KEEP
    slots = quads_ref.shape[1] // KEEP * 4

    def add_list(d, carry):
        puts = []
        for s in range(slots):
            h, g = s // 4, s % 4
            quad = quads_ref[d, h * KEEP : (h + 1) * KEEP, :]
            packed = place_ref[n, d * slots + s]
            to = packed & (LANES - 1)
            moved = pltpu.roll(quad.astype(jnp.float32), (to - g * KEEP) & (LANES - 1), 1)
            row = pl.multiple_of(lax.shift_right_logical(packed, 7), KEEP)
            place = sum_ref.at[pl.ds(row, KEEP)]
            puts.append((place, place[...] + moved, first_lane == to))
        for place, value, mask in puts:
            pltpu.store(place, value, mask=mask)
        return carry

    lax.fori_loop(0, quads_ref.shape[0], add_list, 0, unroll=4)


def last_kernel(place_ref, lows_in, base_in, across_ref, *refs):
    quads, (out_ref, sum_ref, lows_ref, base_ref, sems) = refs[:-5], refs[-5:]
    copies = [
        pltpu.make_async_copy(lows_in, lows_ref, sems.at[0]),
        pltpu.make_async_copy(base_in, base_ref, sems.at[1]),
    ]
    for copy in copies:
        copy.start()
    sum_ref[...] = jnp.zeros_like(sum_ref)
    for n, ref in enumerate(quads):
        add_quads(place_ref, n, ref, sum_ref)
    for copy in copies:
        copy.wait()
    rows = lows_ref.shape[1]
    whole = jnp.concatenate(
        [
            sum_ref[n * rows : (n + 1) * rows, :].astype(jnp.bfloat16)
            for n in range(sum_ref.shape[0] // rows)
        ],
        axis=1,
    )
    mixed = jnp.dot(lows_ref[...], whole, preferred_element_type=jnp.float32)
    update = jnp.dot(
        mixed.astype(jnp.bfloat16), across_ref[...], preferred_element_type=jnp.float32
    )
    out_ref[...] = (base_ref[...] - step_size * update).astype(jnp.bfloat16)


def split_bf16(table):
    top = table.astype(jnp.bfloat16)
    return top, (table - top.astype(np.float32)).astype(jnp.bfloat16)


def room(mib):
    return pltpu.CompilerParams(vmem_limit_bytes=mib * 1024 * 1024)


def vmem(count):
    return [pl.BlockSpec(memory_space=pltpu.VMEM)] * count


def smem(count):
    return [pl.BlockSpec(memory_space=pltpu.SMEM)] * count


def swap(array, axis, bit):
    size = lax.axis_size(axis)
    return lax.ppermute(array, axis, [(i, i ^ bit) for i in range(size)])


def fits(shards, replicas, activations, cotangent, weight_tiles, slots):
    tokens, depth = activations.shape
    width = cotangent.shape[1]
    tiles_here = weight_tiles.shape[0]
    span = span_of(tiles_here, width // TILE)
    return (
        shards == 4
        and replicas == 8
        and tokens % LANES == 0
        and width % tokens == 0
        and width // TILE == 8
        and slots == 8
        and depth % (5 * TILE) == 0
        and tiles_here % 10 == 0
        and tiles_here <= 256
        and slots <= 128
        and span % 2 == 0
        and all((n * tiles_here) // 8 + span <= depth // TILE for n in range(shards))
        and all((n * tiles_here) % 8 + tiles_here <= span * 8 for n in range(shards))
    )


def span_of(tiles_here, col_tiles):
    return 2 * (-(-tiles_here // col_tiles) // 2)


def local(activations, cotangent, next_inputs, weight_tiles, momentum, chosen, counts):
    shards = lax.axis_size("tok")
    replicas = lax.axis_size("replica")
    slots = chosen.shape[-1]
    if not fits(shards, replicas, activations, cotangent, weight_tiles, slots):
        return general(
            activations, cotangent, next_inputs, weight_tiles, momentum, chosen, counts
        )
    return four_shards(
        activations, cotangent, next_inputs, weight_tiles, momentum, chosen, counts
    )


def four_shards(activations, cotangent, next_inputs, weight_tiles, momentum, chosen, counts):
    shards = lax.axis_size("tok")
    replicas = lax.axis_size("replica")
    slots = chosen.shape[-1]
    tokens, depth = activations.shape
    width = cotangent.shape[1]
    tiles_here = weight_tiles.shape[0]
    row_tiles = depth // TILE
    col_tiles = width // TILE
    spans = span_of(tiles_here, col_tiles)
    span_rows = spans * TILE
    scale = 1.0 / math.sqrt(tokens * shards)
    me = lax.axis_index("tok")
    rep = lax.axis_index("replica")
    act = activations.T
    inputs = next_inputs.T
    split, into, split_back, back = tables()

    def place_of(offset):
        return (offset & 1) * 2 + lax.shift_right_logical(offset, 1)

    anywhere = pl.BlockSpec(memory_space=pltpu.HBM)
    share = TILE * TILE // replicas
    listed = chosen[0, 0].astype(jnp.bfloat16)
    pad_rows = -(tiles_here + 1) % 8 + 1
    piece = jnp.concatenate(
        [
            lax.dynamic_slice(weight_tiles, (0, rep * share), (tiles_here, share)),
            jnp.zeros((pad_rows, share), jnp.bfloat16).at[0, :slots].set(listed),
        ],
        axis=0,
    )[None]
    piece_far = swap(piece, "tok", 2)
    pair = jnp.concatenate([piece, piece_far], axis=0)
    pair_near = swap(pair, "tok", 1)
    sent_rows, near_rows = pl.pallas_call(
        functools.partial(prepare_kernel, tiles_here=tiles_here),
        out_shape=[
            jax.ShapeDtypeStruct((span_rows + width, tokens), jnp.bfloat16),
            jax.ShapeDtypeStruct((span_rows, tokens), jnp.bfloat16),
        ],
        in_specs=[anywhere] * 2,
        out_specs=vmem(2),
        scratch_shapes=[pltpu.SemaphoreType.DMA((2 + width // tokens,))],
        name="prepare",
    )(act, cotangent)
    sent_far = swap(sent_rows, "tok", 1)
    mine_far, mine_near = pl.pallas_call(
        functools.partial(mine_kernel, tiles_here=tiles_here, col_tiles=col_tiles),
        out_shape=[jax.ShapeDtypeStruct((span_rows, tokens), jnp.bfloat16)] * 2,
        in_specs=[anywhere],
        out_specs=vmem(2),
        scratch_shapes=[pltpu.SemaphoreType.DMA((2,))],
        name="mine",
    )(act)
    far_chosen = piece_far[0, tiles_here, :slots].astype(jnp.int32)
    near_chosen = pair_near[0, tiles_here, :slots].astype(jnp.int32)
    pieces = jnp.concatenate([pair, pair_near], axis=0)
    sent_near = swap(near_rows, "tok", 1)

    moment = momentum.reshape(tiles_here * KEEP, LANES)
    low = low_rows().astype(np.float32)
    at_once = 5
    sum_rows = place_rows(row_tiles)
    along_high, along_low = split_bf16(np.kron(np.eye(at_once, dtype=np.float32), low))
    across = np.kron(np.eye(col_tiles, dtype=np.float32), low)
    low_shape = jax.ShapeDtypeStruct((slots // 4 * KEEP, LANES), jnp.float32)
    low_mine, low_near = pl.pallas_call(
        functools.partial(factor_lows_kernel, scale=scale, tiles_here=tiles_here),
        out_shape=[low_shape] * 2,
        in_specs=smem(2) + [anywhere] + vmem(8),
        out_specs=vmem(2),
        scratch_shapes=[pltpu.VMEM((row_tiles * KEEP, tokens), jnp.bfloat16)] * 2
        + [
            pltpu.VMEM((col_tiles // 4, row_tiles * KEEP, LANES), jnp.float32),
            pltpu.VMEM((slots, KEEP, LANES), jnp.float32),
            pltpu.SemaphoreType.DMA((slots,)),
        ],
        name="factor_lows",
    )(
        chosen[0, 0], near_chosen, moment, act, cotangent, along_high, along_low,
        *split_bf16(np.ascontiguousarray(across.T)), split, into,
    )
    low_from_near = swap(low_near, "tok", 1)

    grid_scratch = [
        pltpu.VMEM((width // LANES, 2 * TILE, LANES), jnp.float32),
        pltpu.VMEM((spans * col_tiles * KEEP, LANES), jnp.float32),
    ]
    cuts = [tiles_here * 2 // 15, tiles_here // 5]
    cuts.append(tiles_here - sum(cuts))
    far_low, *far_sums = pl.pallas_call(
        functools.partial(far_kernel, scale=scale, spans=spans, tiles_here=tiles_here),
        out_shape=[low_shape]
        + [jax.ShapeDtypeStruct((n * KEEP, LANES), jnp.bfloat16) for n in cuts],
        in_specs=smem(1) + vmem(5),
        out_specs=vmem(1 + len(cuts)),
        scratch_shapes=grid_scratch,
        compiler_params=room(12),
        name="far",
    )(far_chosen, mine_far, cotangent, sent_far, split, into)
    low_from_far = swap(far_low, "tok", 2)
    sums_from = []
    for part in far_sums:
        sums_from.append(swap(part, "tok", 2))

    at = np.arange(low_shape.shape[0])[:, None] // KEEP * 4 + np.arange(LANES) // KEEP
    quads = jnp.where(
        jnp.asarray(at, jnp.int32) < counts[0, 0], low_mine + low_from_near + low_from_far, 0.0
    ).astype(jnp.bfloat16)
    begun = pl.pallas_call(
        functools.partial(own_kernel, scale=scale, spans=spans, tiles_here=tiles_here),
        out_shape=jax.ShapeDtypeStruct(moment.shape, jnp.float32),
        in_specs=smem(1) + [anywhere] + vmem(6 + len(cuts)),
        out_specs=vmem(1)[0],
        scratch_shapes=grid_scratch
        + [pltpu.VMEM(moment.shape, jnp.float32), pltpu.SemaphoreType.DMA((1,))],
        compiler_params=room(16),
        name="own",
    )(
        chosen[0, 0], moment, mine_near, cotangent, sent_far, sent_near, quads, split_back,
        back, *sums_from[:-1],
    )
    new_momentum = pl.pallas_call(
        finish_kernel,
        out_shape=jax.ShapeDtypeStruct(moment.shape, jnp.float32),
        in_specs=vmem(2),
        out_specs=vmem(1)[0],
        compiler_params=room(12),
        name="finish",
    )(begun, sums_from[-1]).reshape(momentum.shape)

    whole = jnp.concatenate(
        [
            lax.dynamic_index_in_dim(pieces, place_of(me ^ n), 0, False)[:tiles_here]
            for n in range(shards)
        ],
        axis=0,
    )
    rows_share = TILE // replicas
    matrix = whole.reshape(row_tiles, col_tiles, rows_share, TILE).transpose(0, 2, 1, 3)
    matrix = matrix.reshape(row_tiles * rows_share, width)
    list_rows = jnp.zeros((8, width), jnp.bfloat16)
    list_rows = list_rows.at[:shards, :slots].set(pieces[:, tiles_here, :slots])
    held = {0: jnp.concatenate([matrix, list_rows], axis=0)}
    held[2] = swap(held[0], "replica", 2)
    held[4] = swap(held[0], "replica", 4)
    held[6] = swap(held[2], "replica", 4)
    near = [held[o] for o in (0, 2, 4, 6)]
    held_all = list(near)
    for h in near:
        held_all.append(swap(h, "replica", 1))
    by_share = inputs.reshape(row_tiles, replicas, rows_share, tokens)
    unchanged, places = pl.pallas_call(
        functools.partial(
            unchanged_kernel, tiles_here=tiles_here, list_row=matrix.shape[0]
        ),
        out_shape=[
            jax.ShapeDtypeStruct((tokens, width), jnp.float32),
            jax.ShapeDtypeStruct((replicas, LANES), jnp.int32),
        ],
        in_specs=[anywhere] + vmem(len(held_all)),
        out_specs=vmem(2),
        scratch_shapes=[
            pltpu.VMEM((replicas, held[0].shape[0] // rows_share, rows_share, tokens), jnp.bfloat16)
        ]
        + [pltpu.SemaphoreType.DMA((replicas,))],
        compiler_params=room(12),
        name="unchanged",
    )(by_share, *held_all)

    lows = pl.pallas_call(
        functools.partial(lows_kernel, span=at_once * TILE),
        out_shape=jax.ShapeDtypeStruct((tokens, sum_rows), jnp.bfloat16),
        in_specs=vmem(3),
        out_specs=vmem(1)[0],
        scratch_shapes=[pltpu.VMEM((sum_rows, tokens), jnp.float32)],
        name="lows",
    )(inputs, along_high, along_low)

    two = jnp.concatenate([quads[None], swap(quads[None], "tok", 2)], axis=0)
    four = jnp.concatenate([two, swap(two, "tok", 1)], axis=0)
    brought = {0: four}
    brought[2] = swap(four, "replica", 2)
    brought[4] = swap(four, "replica", 4)
    brought[6] = swap(brought[2], "replica", 4)
    for o in (0, 2, 4, 6):
        brought[o ^ 1] = swap(brought[o], "replica", 1)
    values = pl.pallas_call(
        last_kernel,
        out_shape=jax.ShapeDtypeStruct((tokens, width), jnp.bfloat16),
        in_specs=smem(1) + [anywhere] * 2 + vmem(1 + len(SHARE_ORDER)),
        out_specs=vmem(1)[0],
        scratch_shapes=[
            pltpu.VMEM((col_tiles // 4 * sum_rows, LANES), jnp.float32),
            pltpu.VMEM(lows.shape, lows.dtype),
            pltpu.VMEM(unchanged.shape, unchanged.dtype),
            pltpu.SemaphoreType.DMA((2,)),
        ],
        compiler_params=room(12),
        name="last",
    )(places, lows, unchanged, across.astype(jnp.bfloat16), *[brought[o] for o in SHARE_ORDER])
    return (values, new_momentum)


def solution(mesh):
    return jax.shard_map(
        local,
        mesh=mesh,
        in_specs=(
            P(("replica", "tok"), None),
            P(("replica", "tok"), None),
            P(("replica", "tok"), None),
            P("tok", None),
            P("replica", "tok", None),
            P("replica", "tok", None),
            P("replica", "tok"),
        ),
        out_specs=(P(("replica", "tok"), None), P("replica", "tok", None)),
        check_vma=False,
    )
```
